128 devices in a mesh: group: 8 (over y, core), member: 16 (over z, x).
Axes of the slice: x: 4, y: 4, z: 4, core: 2. Of those that a mesh axis runs over, the one named last changes fastest.
Arguments:
- hidden: bfloat16 [49152, 3584], P(('group', 'member')), may hold values from -30 to 30
- projection: bfloat16 [3584, 1024], replicated, may hold values from -0.09375 to 0.09375
- inv_temp: float32 [1], replicated, may hold values from 10 to 80
- partners: int32 [128, 12], P(('group', 'member')), may hold values from 0 to 127, as said below
- positives: int32 [49152], P(('group', 'member')), may hold values from 0 to 49151, as said below
Outputs:
- loss: float32 [], replicated
- grad_hidden: bfloat16 [49152, 3584], P(('group', 'member'))
- grad_proj: float32 [3584, 1024], P(('group', 'member'))
The draws below stay inside these ranges and needn't reach their ends.
Inputs may be any that keep to these rules, and one draw needn't show every extreme that they name: Block ids are numbered in row order. partners[b] are 12 distinct blocks of b's own group of 16 consecutive blocks, none equal to b; within a group they are b's index in the group XORed with 12 distinct nonzero offsets common to that group, so b lists c exactly when c lists b. positives pairs the rows of each block among themselves: positives_i lies in i's block, differs from i, and positives of positives_i is i.
All inputs are finite; a program needn't handle non-finite values.
Results may differ from the reference program's by a relative error of at most 0.006.
Values may be sent and summed in bfloat16 or wider, within the bound.
No kernel may reach another device: no remote copies, remote signals or barrier semaphores. Data moves between devices by JAX's collectives and lax.ppermute only.
A program may use at most 128 MiB of HBM per device.

```python
import jax
import jax.numpy as jnp
from jax import lax

HID = 3584
D = 1024
BLOCK = 384
PARTNERS = 12
GROUP_BLOCKS = 16
ROWS = 49152


def draw_inv_temp(key, part):
    return jax.random.uniform(key, (1,), jnp.float32, 10.0, 30.0)


def draw_partners(key, part):
    blocks = ROWS // BLOCK
    groups = blocks // GROUP_BLOCKS
    subkeys = jax.random.split(key, groups)
    offsets = jax.vmap(lambda subkey: jax.random.permutation(subkey, GROUP_BLOCKS - 1))(subkeys)[:, :PARTNERS] + 1
    inside = jnp.arange(GROUP_BLOCKS, dtype=jnp.int32)
    partner_ids = jnp.arange(groups, dtype=jnp.int32)[:, None, None] * GROUP_BLOCKS + jnp.bitwise_xor(inside[None, :, None], offsets.astype(jnp.int32)[:, None, :])
    return partner_ids.reshape(blocks, PARTNERS).astype(jnp.int32)


def draw_positives(key, part):
    blocks = ROWS // BLOCK
    subkeys = jax.random.split(key, blocks)
    orders = jax.vmap(lambda subkey: jax.random.permutation(subkey, BLOCK))(subkeys).astype(jnp.int32)
    swapped = orders.reshape(blocks, BLOCK // 2, 2)[:, :, ::-1].reshape(blocks, BLOCK)
    block_ids = jnp.arange(blocks, dtype=jnp.int32)[:, None]
    paired = jnp.zeros((blocks, BLOCK), jnp.int32).at[block_ids, orders].set(swapped)
    return (paired + block_ids * BLOCK).reshape(-1).astype(jnp.int32)


def draw_hidden(key, part):
    blocks = ROWS // BLOCK
    paired = draw_positives(key, part)
    first_key = jax.random.fold_in(key, 101)
    second_key = jax.random.fold_in(key, 202)
    spike_key = jax.random.fold_in(key, 303)
    noise_own = jnp.clip(jax.random.normal(first_key, (ROWS, HID), jnp.float32), -6.0, 6.0)
    noise_pair = jnp.clip(jax.random.normal(second_key, (ROWS, HID), jnp.float32), -6.0, 6.0)
    high_mix = 0.85
    shared = (noise_pair + noise_pair[paired]) * 0.7071
    block_of = jnp.arange(ROWS, dtype=jnp.int32) // BLOCK
    ramp = block_of.astype(jnp.float32) / float(max(blocks - 1, 1))
    mixing = (high_mix * ramp)[:, None]
    values = jnp.sqrt(1.0 - mixing * mixing) * noise_own + mixing * shared
    order = jax.random.permutation(spike_key, blocks).astype(jnp.int32)
    col_block = jnp.arange(HID, dtype=jnp.int32) // (HID // blocks)
    spiked = order[block_of][:, None] == col_block[None, :]
    values = jnp.where(spiked, 4.0 * values, values)
    return values.astype(jnp.bfloat16)


def noise(rng, dims, scale, limit, kind=jnp.bfloat16):
    array = scale * jax.random.normal(rng, dims, jnp.float32)
    return jnp.clip(array, min=-limit, max=limit).astype(kind)


def setup_inputs(seed: int = 0) -> dict:
    streams_of = jax.random.split(jax.random.key(seed), 6)
    hidden = draw_hidden(jax.random.fold_in(streams_of[5], 71), 0)
    projection = noise(streams_of[1], (HID, D), HID ** -0.5, 0.09375)
    inv_temp = draw_inv_temp(jax.random.fold_in(streams_of[5], 71), 0)
    partners = draw_partners(jax.random.fold_in(streams_of[5], 71), 0)
    positives = draw_positives(jax.random.fold_in(streams_of[5], 71), 0)
    return dict(hidden=hidden, projection=projection, inv_temp=inv_temp, partners=partners, positives=positives)


epsilon = 1e-06

def reference(hidden, projection, inv_temp, partners, positives):
    projected = jnp.dot(hidden, projection, preferred_element_type=jnp.float32)
    lengths = jnp.sqrt(lax.optimization_barrier(jnp.sum(projected * projected, axis=1, keepdims=True)) + epsilon)
    unit_rows = projected / lengths
    unit_low = unit_rows.astype(jnp.bfloat16)
    blocks = ROWS // BLOCK
    stacked = unit_low.reshape(blocks, BLOCK, D)
    scale = inv_temp[0]
    diagonal = jnp.eye(BLOCK, dtype=bool)
    first = (jnp.arange(PARTNERS + 1) == 0)[:, None, None]
    self_mask = first & diagonal[None]
    local_pos = (positives % BLOCK).reshape(blocks, BLOCK)
    columns = jnp.arange(BLOCK)

    def tile_scores(index):
        chosen = jnp.concatenate([index[None].astype(jnp.int32), partners[index].astype(jnp.int32)])
        others = stacked[chosen]
        scores = scale * jnp.einsum('id,pjd->pij', stacked[index].astype(jnp.float32), others.astype(jnp.float32))
        scores = jnp.where(self_mask, -jnp.inf, scores)
        return (scores, chosen, others)

    def row_totals(index):
        scores, chosen, others = tile_scores(index)
        highest = lax.optimization_barrier(jnp.max(scores, axis=(0, 2)))
        return highest + jnp.log(lax.optimization_barrier(jnp.sum(jnp.exp(scores - highest[None, :, None]), axis=(0, 2))))
    log_totals = lax.map(row_totals, jnp.arange(blocks))
    pos_scores = scale * lax.optimization_barrier(jnp.sum(unit_low.astype(jnp.float32) * unit_low[positives].astype(jnp.float32), axis=1))
    loss = jnp.mean(log_totals.reshape(-1) - pos_scores)

    def block_grad(index):
        scores, chosen, others = tile_scores(index)
        row_prob = jnp.exp(scores - log_totals[index][None, :, None])
        col_prob = jnp.exp(scores - log_totals[chosen][:, None, :])
        target = first & (columns[None, None, :] == local_pos[index][:, None][None])
        weights = (row_prob + col_prob - 2.0 * target).astype(jnp.bfloat16)
        return scale * jnp.einsum('pij,pjd->id', weights.astype(jnp.float32), others.astype(jnp.float32))
    grad_unit = lax.map(block_grad, jnp.arange(blocks)).reshape(ROWS, D)
    along = lax.optimization_barrier(jnp.sum(unit_rows * grad_unit, axis=1, keepdims=True))
    grad_projected = ((grad_unit - unit_rows * along) / lengths).astype(jnp.bfloat16)
    grad_hidden = jnp.dot(grad_projected, projection.T, preferred_element_type=jnp.float32).astype(jnp.bfloat16)
    grad_proj = jnp.dot(hidden.T, grad_projected, preferred_element_type=jnp.float32)
    return (loss, grad_hidden, grad_proj)
```

```python
import jax
import jax.numpy as jnp
from jax import lax
from jax.sharding import Mesh, PartitionSpec as P

epsilon = 1e-06
shift = 3.0
AXES = ("y", "core", "z", "x")


def send(array, axis, step):
    return lax.ppermute(array, axis, [(i, (i + step) % 4) for i in range(4)])


def swap(array):
    return lax.ppermute(array, "core", [(0, 1), (1, 0)])


def ring_gather(block, axis):
    half = block.shape[0] // 2
    back = send(block, axis, 1)
    ahead = send(block, axis, -1)
    far_top = send(back[:half], axis, 1)
    far_bottom = send(ahead[half:], axis, -1)
    return [block, back, far_top, far_bottom, ahead]


def ring_total(parts, axis):
    total = parts
    for d in (1, 2, 3):
        seen = send(parts, axis, -d)
        total = total + jnp.roll(seen, -d, axis=0)
    return total


def total_over(value, axis):
    return value + send(value, axis, 1) + send(value, axis, 2) + send(value, axis, 3)


def per_device(hidden, projection, inv_temp, partners, positives):
    rows = hidden.shape[0]
    width = projection.shape[1]
    half = width // 2
    scale = inv_temp[0]
    iy, ic = lax.axis_index("y"), lax.axis_index("core")
    iz, ix = lax.axis_index("z"), lax.axis_index("x")
    mine = iz * 4 + ix

    projected = jnp.dot(hidden, projection, preferred_element_type=jnp.float32)
    lengths = jnp.sqrt(jnp.sum(projected * projected, axis=1, keepdims=True) + epsilon)
    unit_rows = projected / lengths
    unit_low = unit_rows.astype(jnp.bfloat16)

    eighth = hidden.shape[1] // 8
    def columns_of(place):
        return lax.dynamic_slice_in_dim(hidden, place * (2 * eighth), 2 * eighth, axis=1)
    by_y = [columns_of(iy)] + [send(columns_of((iy + d) % 4), "y", d) for d in (1, 2, 3)]
    by_y = jnp.stack(by_y)
    first_core = ic == 0
    low, high = by_y[:, :, :eighth], by_y[:, :, eighth:]
    kept = jnp.where(first_core, low, high)
    other = swap(jnp.where(first_core, high, low))
    hidden_part = jnp.concatenate([kept, other], axis=0).reshape(8 * rows, eighth)

    row_units = jnp.concatenate(ring_gather(unit_low, "x"), axis=0)
    col_units = jnp.concatenate(ring_gather(unit_low, "z"), axis=0)

    offsets = (partners[0] % 16) ^ mine
    back = jnp.arange(4)
    row_ids = iz * 4 + (ix - back) % 4
    col_ids = ((iz - back) % 4) * 4 + ix
    apart = row_ids[:, None] ^ col_ids[None, :]
    active = jnp.any(apart[:, :, None] == offsets, axis=2) | (apart == 0)

    scores = scale * lax.dot_general(
        row_units, col_units, (((1,), (1,)), ((), ())), preferred_element_type=jnp.float32
    )
    scores = scores.reshape(4, rows, 4, rows)
    columns = jnp.arange(rows)
    own_tile = ((back[:, None] == 0) & (back[None, :] == 0))[:, None, :, None]
    self_mask = own_tile & (columns[:, None] == columns[None, :])[None, :, None, :]
    keep = active[:, None, :, None] & ~self_mask
    powers = jnp.where(keep, jnp.exp(scores - shift), 0.0)
    row_totals = ring_total(jnp.sum(powers, axis=(2, 3)), "x")
    col_totals = ring_total(jnp.sum(powers, axis=(0, 1)), "z")

    local_pos = positives % rows
    target = columns[None, :] == local_pos[:, None]
    pos_scores = jnp.sum(jnp.where(target, scores[0, :, 0, :], 0.0), axis=1)
    row_loss = jnp.sum(shift + jnp.log(row_totals[0]) - pos_scores)
    total = jnp.full((8, 128), row_loss)
    total = total + swap(total)
    for axis in ("y", "z", "x"):
        total = total_over(total, axis)
    loss = total[0, 0] / (128 * rows)

    both = (1.0 / row_totals)[:, :, None, None] + (1.0 / col_totals)[None, None, :, :]
    own_target = own_tile & target[None, :, None, :]
    weights = (powers * both - 2.0 * own_target).astype(jnp.bfloat16).reshape(4 * rows, 4 * rows)
    by_rows = jnp.dot(weights, col_units[:, :half], preferred_element_type=jnp.float32)
    by_cols = lax.dot_general(
        weights, row_units[:, half:], (((0,), (0,)), ((), ())), preferred_element_type=jnp.float32
    )
    halves = []
    for part, axis in ((by_rows, "x"), (by_cols, "z")):
        part = part.reshape(4, rows, half)
        total_part = part[0]
        for d in (1, 2, 3):
            total_part = total_part + send(part[d].astype(jnp.bfloat16), axis, -d).astype(jnp.float32)
        halves.append(total_part)
    grad_unit = scale * jnp.concatenate(halves, axis=1)
    along = jnp.sum(unit_rows * grad_unit, axis=1, keepdims=True)
    grad_projected = ((grad_unit - unit_rows * along) / lengths).astype(jnp.bfloat16)
    grad_hidden = lax.dot_general(
        grad_projected, projection, (((1,), (1,)), ((), ())), preferred_element_type=jnp.float32
    ).astype(jnp.bfloat16)

    gathered = jnp.concatenate(ring_gather(grad_projected, "y"), axis=0)
    gathered = jnp.concatenate([gathered, swap(gathered)], axis=0)
    part = lax.dot_general(
        hidden_part, gathered, (((0,), (0,)), ((), ())), preferred_element_type=jnp.float32
    )
    part = part.astype(jnp.bfloat16).reshape(16, eighth // 16, width)
    arrived = lax.all_to_all(part, ("z", "x"), 0, 0)
    grad_proj = jnp.sum(arrived.astype(jnp.float32), axis=0)
    return (loss, grad_hidden, grad_proj)


def solution(mesh):
    split = Mesh(mesh.devices.reshape(4, 2, 4, 4), AXES)
    return jax.shard_map(
        per_device,
        mesh=split,
        in_specs=(P(AXES, None), P(), P(), P(AXES, None), P(AXES)),
        out_specs=(P(), P(AXES, None), P(AXES, None)),
        check_vma=False,
    )
```

```python
import functools

import jax
import jax.numpy as jnp
from jax import lax
from jax.experimental import pallas as pl
from jax.experimental.pallas import tpu as pltpu
from jax.sharding import Mesh, PartitionSpec as P

epsilon = 1e-06
shift = 3.0
AXES = ("y", "core", "z", "x")
NEAR = [(0, 0), (0, 1), (0, 3), (1, 0), (1, 1), (1, 3), (3, 0), (3, 1), (3, 3)]
FAR = [(0, 2), (1, 2), (3, 2), (2, 0), (2, 1), (2, 2), (2, 3)]


def send(array, axis, step):
    return lax.ppermute(array, axis, [(i, (i + step) % 4) for i in range(4)])


def swap(array):
    return lax.ppermute(array, "core", [(0, 1), (1, 0)])


def ring_gather(top, bottom, axis):
    back_top = send(top, axis, 1)
    ahead_bottom = send(bottom, axis, -1)
    back_bottom = send(bottom, axis, 1)
    ahead_top = send(top, axis, -1)
    far_top = send(back_top, axis, 1)
    far_bottom = send(ahead_bottom, axis, -1)
    return (back_top, back_bottom), (far_top, far_bottom), (ahead_top, ahead_bottom)


def ring_total(parts, axis):
    total = parts
    for d in (1, 2, 3):
        seen = send(parts, axis, -d)
        total = total + jnp.roll(seen, -d, axis=0)
    return total


def total_over(value, axis):
    return value + send(value, axis, 1) + send(value, axis, 2) + send(value, axis, 3)


def ring_scatter(own, near, far, ahead, axis):
    half = far.shape[0] // 2
    top = send(far[:half], axis, -1)
    bottom = send(far[half:], axis, 1)
    near_top = (near[:half] + top.astype(jnp.float32)).astype(jnp.bfloat16)
    near = jnp.concatenate([near_top, near[half:].astype(jnp.bfloat16)], axis=0)
    ahead_bottom = (ahead[half:] + bottom.astype(jnp.float32)).astype(jnp.bfloat16)
    ahead = jnp.concatenate([ahead[:half].astype(jnp.bfloat16), ahead_bottom], axis=0)
    from_next = send(near, axis, -1)
    from_last = send(ahead, axis, 1)
    return own + from_next.astype(jnp.float32) + from_last.astype(jnp.float32)


def target_of(pos):
    rows = pos.shape[0]
    return lax.broadcasted_iota(jnp.int32, (rows, rows), 1) == pos


def score_kernel(tiles, names, *refs):
    active, scale, pos = refs[:3]
    row_refs = dict(zip(names, refs[3 : 3 + len(names)]))
    col_refs = dict(zip(names, refs[3 + len(names) : 3 + 2 * len(names)]))
    powers, row_sums, col_sums, pos_scores = refs[3 + 2 * len(names) :]
    rows = pos.shape[0]
    row_sums[...] = jnp.zeros_like(row_sums)
    col_sums[...] = jnp.zeros_like(col_sums)
    pos_scores[...] = jnp.zeros_like(pos_scores)
    factor = scale[0]
    for place, (dx, dz) in enumerate(tiles):
        @pl.when(active[4 * dx + dz] == 1)
        def _():
            scores = factor * lax.dot_general(
                row_refs[dx][...],
                col_refs[dz][...],
                (((1,), (1,)), ((), ())),
                preferred_element_type=jnp.float32,
            )
            power = jnp.exp(scores - shift)
            if (dx, dz) == (0, 0):
                here = lax.broadcasted_iota(jnp.int32, (rows, rows), 0)
                there = lax.broadcasted_iota(jnp.int32, (rows, rows), 1)
                power = jnp.where(here == there, 0.0, power)
                hit = jnp.where(target_of(pos[...]), scores, 0.0)
                pos_scores[...] = hit[:, :128] + hit[:, 128:256] + hit[:, 256:]
            powers[place] = power.astype(jnp.bfloat16)
            row_sums[dx] += power[:, :128] + power[:, 128:256] + power[:, 256:]
            col_sums[dz] += jnp.sum(power.reshape(rows // 8, 8, rows), axis=0)


def score_tiles(tiles, active, scale, pos, row_blocks, col_blocks):
    names = sorted({d for tile in tiles for d in tile})
    rows = pos.shape[0]
    smem = pl.BlockSpec(memory_space=pltpu.SMEM)
    vmem = pl.BlockSpec(memory_space=pltpu.VMEM)
    return pl.pallas_call(
        functools.partial(score_kernel, tiles, names),
        out_shape=(
            jax.ShapeDtypeStruct((len(tiles), rows, rows), jnp.bfloat16),
            jax.ShapeDtypeStruct((4, rows, 128), jnp.float32),
            jax.ShapeDtypeStruct((4, 8, rows), jnp.float32),
            jax.ShapeDtypeStruct((rows, 128), jnp.float32),
        ),
        in_specs=[smem, smem] + [vmem] * (1 + 2 * len(names)),
        out_specs=(vmem,) * 4,
        compiler_params=pltpu.CompilerParams(vmem_limit_bytes=48 << 20),
        name="scores",
    )(active, scale, pos, *[row_blocks[d] for d in names], *[col_blocks[d] for d in names])


def grad_kernel(chunks, active, pos, row_inv, col_inv, near, far, r0, r1, r2, r3, c0, c1, c2, c3, *refs):
    row_refs, col_refs = (r0, r1, r2, r3), (c0, c1, c2, c3)
    by_row = dict(zip(chunks, refs[: len(chunks)]))
    by_col = dict(zip(chunks, refs[len(chunks) : 2 * len(chunks)]))
    sums = refs[2 * len(chunks)]
    rows = pos.shape[0]
    half = r0.shape[1] // 2
    sums[...] = jnp.zeros_like(sums)
    for dx in range(4):
        for dz in range(4):
            if dx not in chunks and dz not in chunks:
                continue
            source, place = (near, NEAR.index((dx, dz))) if (dx, dz) in NEAR else (far, FAR.index((dx, dz)))

            @pl.when(active[4 * dx + dz] == 1)
            def _():
                inv = row_inv[dx]
                both = jnp.concatenate([inv, inv, inv], axis=1) + col_inv[dz]
                weight = source[place].astype(jnp.float32) * both
                if (dx, dz) == (0, 0):
                    weight = weight - jnp.where(target_of(pos[...]), 2.0, 0.0)
                weight = weight.astype(jnp.bfloat16)
                if dx in chunks:
                    sums[chunks.index(dx)] += jnp.dot(
                        weight, col_refs[dz][:, :half], preferred_element_type=jnp.float32
                    )
                if dz in chunks:
                    sums[len(chunks) + chunks.index(dz)] += lax.dot_general(
                        weight,
                        row_refs[dx][:, half:],
                        (((0,), (0,)), ((), ())),
                        preferred_element_type=jnp.float32,
                    )
    for place, d in enumerate(chunks):
        by_row[d][...] = sums[place].astype(by_row[d].dtype)
        by_col[d][...] = sums[len(chunks) + place].astype(by_col[d].dtype)


def grad_chunks(chunks, kind, active, pos, row_inv, col_inv, near, far, row_blocks, col_blocks):
    rows, width = row_blocks[0].shape
    smem = pl.BlockSpec(memory_space=pltpu.SMEM)
    vmem = pl.BlockSpec(memory_space=pltpu.VMEM)
    made = pl.pallas_call(
        functools.partial(grad_kernel, chunks),
        out_shape=tuple(jax.ShapeDtypeStruct((rows, width // 2), kind) for _ in range(2 * len(chunks))),
        in_specs=[smem] + [vmem] * 13,
        out_specs=(vmem,) * (2 * len(chunks)),
        scratch_shapes=[pltpu.VMEM((2 * len(chunks), rows, width // 2), jnp.float32)],
        compiler_params=pltpu.CompilerParams(vmem_limit_bytes=48 << 20),
        name="weights",
    )(active, pos, row_inv, col_inv, near, far, *row_blocks, *col_blocks)
    return dict(zip(chunks, made[: len(chunks)])), dict(zip(chunks, made[len(chunks) :]))


def per_device(hidden, projection, inv_temp, partners, positives):
    rows = hidden.shape[0]
    width = projection.shape[1]
    half = width // 2
    iy, ic = lax.axis_index("y"), lax.axis_index("core")
    iz, ix = lax.axis_index("z"), lax.axis_index("x")
    mine = iz * 4 + ix

    offsets = (partners[0] % 16) ^ mine
    back = jnp.arange(4)
    row_ids = iz * 4 + (ix - back) % 4
    col_ids = ((iz - back) % 4) * 4 + ix
    apart = (row_ids[:, None] ^ col_ids[None, :]).reshape(16)
    active = (jnp.any(apart[:, None] == offsets[None, :], axis=1) | (apart == 0)).astype(jnp.int32)
    pos = (positives % rows)[:, None]

    projected = jnp.dot(hidden, projection, preferred_element_type=jnp.float32)
    lengths = jnp.sqrt(jnp.sum(projected * projected, axis=1, keepdims=True) + epsilon)
    unit_rows = projected / lengths
    unit_low = unit_rows.astype(jnp.bfloat16)

    top, bottom = unit_low[: rows // 2], unit_low[rows // 2 :]
    x_back, x_far, x_ahead = ring_gather(top, bottom, "x")
    z_back, z_far, z_ahead = ring_gather(top, bottom, "z")

    fourth = hidden.shape[1] // 4
    def columns_of(place):
        return lax.dynamic_slice_in_dim(hidden, place * fourth, fourth, axis=1)
    by_y = [columns_of(iy)] + [send(columns_of((iy + d) % 4), "y", d) for d in (1, 2, 3)]
    x_far, z_far, by_y = lax.optimization_barrier((x_far, z_far, by_y))
    own_hidden = jnp.concatenate(by_y, axis=0)
    other_hidden = swap(own_hidden)

    def whole(pieces):
        return jnp.concatenate(pieces, axis=0)
    row_blocks = {0: unit_low, 1: whole(x_back), 3: whole(x_ahead)}
    col_blocks = {0: unit_low, 1: whole(z_back), 3: whole(z_ahead)}
    near, near_rows, near_cols, hits = score_tiles(NEAR, active, inv_temp, pos, row_blocks, col_blocks)
    row_blocks[2], col_blocks[2] = whole(x_far), whole(z_far)
    far, far_rows, far_cols, _ = score_tiles(FAR, active, inv_temp, pos, row_blocks, col_blocks)

    row_totals = ring_total(jnp.sum(near_rows + far_rows, axis=2), "x")
    col_totals = ring_total(jnp.sum(near_cols + far_cols, axis=1), "z")
    row_inv = jnp.broadcast_to((1.0 / row_totals)[:, :, None], (4, rows, 128))
    col_inv = (1.0 / col_totals)[:, None, :]
    row_inv, col_inv, other_hidden = lax.optimization_barrier((row_inv, col_inv, other_hidden))

    row_list = [row_blocks[d] for d in range(4)]
    col_list = [col_blocks[d] for d in range(4)]
    shared = (active, pos, row_inv, col_inv, near, far, row_list, col_list)
    far_row, far_col = grad_chunks((2,), jnp.bfloat16, *shared)
    by_row, by_col = grad_chunks((1, 3, 0), jnp.float32, *shared)
    halves = [
        ring_scatter(by_row[0], by_row[1], far_row[2], by_row[3], "x"),
        ring_scatter(by_col[0], by_col[1], far_col[2], by_col[3], "z"),
    ]
    grad_unit = inv_temp[0] * jnp.concatenate(halves, axis=1)
    along = jnp.sum(unit_rows * grad_unit, axis=1, keepdims=True)
    grad_projected = ((grad_unit - unit_rows * along) / lengths).astype(jnp.bfloat16)
    grad_hidden = lax.dot_general(
        grad_projected, projection, (((1,), (1,)), ((), ())), preferred_element_type=jnp.float32
    ).astype(jnp.bfloat16)

    row_loss = jnp.sum(shift + jnp.log(row_totals[0])) - jnp.sum(hits)
    total = jnp.full((8, 128), row_loss)
    total = total + swap(total)
    for axis in ("y", "z", "x"):
        total = total_over(total, axis)

    left, right = grad_projected[:, :half], grad_projected[:, half:]
    kept = jnp.where(ic == 0, left, right)
    other = swap(jnp.where(ic == 0, right, left))
    y_back, y_far, y_ahead = ring_gather(kept, other, "y")
    own_rows = jnp.concatenate([kept, y_back[0], y_far[0], y_ahead[0]], axis=0)
    other_rows = jnp.concatenate([other, y_back[1], y_far[1], y_ahead[1]], axis=0)
    own_rows, other_rows, grad_hidden, total = lax.optimization_barrier(
        (own_rows, other_rows, grad_hidden, total)
    )
    loss = total[0, 0] / (128 * rows)
    over_rows = (((0,), (0,)), ((), ()))
    part = lax.dot_general(own_hidden, own_rows, over_rows, preferred_element_type=jnp.float32)
    part = part + lax.dot_general(other_hidden, other_rows, over_rows, preferred_element_type=jnp.float32)
    part = part.astype(jnp.bfloat16).reshape(32, fourth // 32, half)
    arrived = lax.all_to_all(part, ("core", "z", "x"), 0, 0)
    sums = jnp.sum(arrived.reshape(2, 16, fourth // 32, half).astype(jnp.float32), axis=1)
    grad_proj = jnp.concatenate([sums[0], sums[1]], axis=1)
    return (loss, grad_hidden, grad_proj)


def solution(mesh):
    split = Mesh(mesh.devices.reshape(4, 2, 4, 4), AXES)
    return jax.shard_map(
        per_device,
        mesh=split,
        in_specs=(P(AXES, None), P(), P(), P(AXES, None), P(AXES)),
        out_specs=(P(), P(AXES, None), P(AXES, None)),
        check_vma=False,
    )
```

```python
import functools

import jax
import jax.numpy as jnp
from jax import lax
from jax.experimental import pallas as pl
from jax.experimental.pallas import tpu as pltpu
from jax.sharding import Mesh, PartitionSpec as P

epsilon = 1e-06
shift = 3.0
AXES = ("y", "core", "z", "x")
NEAR = [(0, 0), (0, 1), (0, 3), (1, 0), (1, 1), (1, 3), (3, 0), (3, 1), (3, 3)]
FAR = [(0, 2), (1, 2), (3, 2), (2, 0), (2, 1), (2, 2), (2, 3)]


def send(array, axis, step):
    return lax.ppermute(array, axis, [(i, (i + step) % 4) for i in range(4)])


def swap(array):
    return lax.ppermute(array, "core", [(0, 1), (1, 0)])


def ring_gather(block, axis):
    half = block.shape[0] // 2
    back = send(block, axis, 1)
    ahead = send(block, axis, -1)
    far_top = send(back[:half], axis, 1)
    far_bottom = send(ahead[half:], axis, -1)
    return (back,), (far_top, far_bottom), (ahead,)


def ring_total(parts, axis):
    total = parts
    for d in (1, 2, 3):
        seen = send(parts, axis, -d)
        total = total + jnp.roll(seen, -d, axis=0)
    return total


def total_over_y(value):
    for bit in (1, 2):
        value = value + lax.ppermute(value, "y", [(i, i ^ bit) for i in range(4)])
    return value


def target_of(pos):
    rows = pos.shape[0]
    return lax.broadcasted_iota(jnp.int32, (rows, rows), 1) == pos


def score_kernel(tiles, names, pieces, final, *refs):
    active, scale, pos = refs[:3]
    count = sum(pieces)
    row_in, col_in = refs[3 : 3 + count], refs[3 + count : 3 + 2 * count]
    outs = refs[3 + 2 * count :]
    powers, row_sums, col_sums = outs[:3]
    row_units, col_units = outs[-2:]
    rows = pos.shape[0]
    row_sums[...] = jnp.zeros_like(row_sums)
    col_sums[...] = jnp.zeros_like(col_sums)
    for sources, target in ((row_in, row_units), (col_in, col_units)):
        at = 0
        for place, many in enumerate(pieces):
            cut = rows // many
            for part in range(many):
                target[place, cut * part : cut * (part + 1)] = sources[at][...]
                at += 1
    factor = scale[0]
    for place, (dx, dz) in enumerate(tiles):
        scores = factor * lax.dot_general(
            row_units[names.index(dx)],
            col_units[names.index(dz)],
            (((1,), (1,)), ((), ())),
            preferred_element_type=jnp.float32,
        )
        power = jnp.exp(scores - shift)
        if (dx, dz) == (0, 0):
            here = lax.broadcasted_iota(jnp.int32, (rows, rows), 0)
            there = lax.broadcasted_iota(jnp.int32, (rows, rows), 1)
            power = jnp.where(here == there, 0.0, power)
            hit = jnp.where(target_of(pos[...]), scores, 0.0)
            outs[3][...] = hit[:, :128] + hit[:, 128:256] + hit[:, 256:]
        else:
            power = power * active[4 * dx + dz]
        powers[place] = power.astype(jnp.bfloat16)
        row_sums[dx] += power[:, :128] + power[:, 128:256] + power[:, 256:]
        col_sums[dz] += jnp.sum(power.reshape(rows // 8, 8, rows), axis=0)
    if final:
        half = row_units.shape[2] // 2
        for place, d in enumerate(names):
            outs[3][rows * d : rows * (d + 1)] = row_units[place, :, half:]
            outs[4][rows * d : rows * (d + 1)] = col_units[place, :, :half]


def score_tiles(tiles, final, active, scale, pos, row_pieces, col_pieces):
    names = sorted({d for tile in tiles for d in tile})
    rows = pos.shape[0]
    width = row_pieces[0][0].shape[1]
    smem = pl.BlockSpec(memory_space=pltpu.SMEM)
    vmem = pl.BlockSpec(memory_space=pltpu.VMEM)
    out_shape = [
        jax.ShapeDtypeStruct((len(tiles), rows, rows), jnp.bfloat16),
        jax.ShapeDtypeStruct((4, rows, 128), jnp.float32),
        jax.ShapeDtypeStruct((4, 8, rows), jnp.float32),
    ]
    if final:
        out_shape += [jax.ShapeDtypeStruct((4 * rows, width // 2), jnp.bfloat16)] * 2
    else:
        out_shape += [jax.ShapeDtypeStruct((rows, 128), jnp.float32)]
    block = pltpu.VMEM((len(names), rows, width), jnp.bfloat16)
    pieces = [len(row_pieces[d]) for d in names]
    return pl.pallas_call(
        functools.partial(score_kernel, tiles, names, pieces, final),
        out_shape=tuple(out_shape),
        in_specs=[smem, smem] + [vmem] * (1 + 2 * sum(pieces)),
        out_specs=(vmem,) * len(out_shape),
        scratch_shapes=[block, block],
        compiler_params=pltpu.CompilerParams(vmem_limit_bytes=48 << 20),
        cost_estimate=pl.CostEstimate(
            flops=len(tiles) * 2 * rows * rows * width,
            transcendentals=len(tiles) * rows * rows,
            bytes_accessed=16 << 20,
        ),
        name="scores",
    )(
        active, scale, pos,
        *[piece for d in names for piece in row_pieces[d]],
        *[piece for d in names for piece in col_pieces[d]],
    )


def weight_tile(source, place, dx, dz, row_inv, col_inv):
    inv = row_inv[dx]
    return source[place].astype(jnp.float32) * (jnp.concatenate([inv, inv, inv], axis=1) + col_inv[dz])


def product(left, right):
    return jnp.dot(left, right, preferred_element_type=jnp.float32)


def product_over_rows(left, right):
    return lax.dot_general(left, right, (((0,), (0,)), ((), ())), preferred_element_type=jnp.float32)


def far_kernel(row_inv, col_inv, far, rows_right, cols_left, far_row, far_col, wide, tall):
    rows = far.shape[1]
    for place, (dx, dz) in enumerate(FAR):
        weight = weight_tile(far, place, dx, dz, row_inv, col_inv).astype(jnp.bfloat16)
        if dx == 2:
            wide[:, rows * dz : rows * (dz + 1)] = weight
        if dz == 2:
            tall[rows * dx : rows * (dx + 1)] = weight
    far_row[...] = product(wide[...], cols_left[...]).astype(far_row.dtype)
    far_col[...] = product_over_rows(tall[...], rows_right[...]).astype(far_col.dtype)


def own_kernel(pos, row_inv, col_inv, near, wide, tall, rows_right, cols_left, by_row, by_col, weights):
    rows = pos.shape[0]
    weights[2 * rows : 3 * rows] = wide[...]
    weights[:, 2 * rows : 3 * rows] = tall[...]
    for place, (dx, dz) in enumerate(NEAR):
        weight = weight_tile(near, place, dx, dz, row_inv, col_inv)
        if (dx, dz) == (0, 0):
            weight = weight - jnp.where(target_of(pos[...]), 2.0, 0.0)
        weights[rows * dx : rows * (dx + 1), rows * dz : rows * (dz + 1)] = weight.astype(jnp.bfloat16)
    by_row[...] = product(weights[:rows], cols_left[...])
    by_col[...] = product_over_rows(weights[:, :rows], rows_right[...])


def near_kernel(weights, rows_right, cols_left, x_top, x_bottom, z_top, z_bottom, *outs):
    rows = weights.shape[0] // 4
    cut = rows // 2
    for place, d in enumerate((1, 3)):
        span = slice(cut) if d == 1 else slice(cut, rows)
        by_row = product(weights[rows * d : rows * (d + 1)], cols_left[...])
        by_col = product_over_rows(weights[:, rows * d : rows * (d + 1)], rows_right[...])
        for out, made, seen in (
            (outs[place], by_row, (x_top, x_bottom)[place]),
            (outs[2 + place], by_col, (z_top, z_bottom)[place]),
        ):
            out[...] = made.astype(out.dtype)
            out[span] = (made[span] + seen[...].astype(jnp.float32)).astype(out.dtype)


def gather_kernel(names, places, hidden_own, hidden_other, *refs):
    own, other = refs[: len(names)], refs[len(names) : 2 * len(names)]
    total = jnp.zeros((hidden_own.shape[2], own[0].shape[1]), jnp.float32)
    for k, d in enumerate(names):
        total += product_over_rows(hidden_own[places[d]], own[k][...])
        total += product_over_rows(hidden_other[places[d]], other[k][...])
    refs[-1][...] = total


def last_kernel(places, hidden_own, hidden_other, own, other, first, spare, out, total):
    total[...] = (
        first[...]
        + product_over_rows(hidden_own[places[2]], own[...])
        + product_over_rows(hidden_other[places[2]], other[...])
    )
    count, padded = out.shape[:2]
    rows = padded - spare.shape[0]
    for k in range(count):
        out[k, :rows] = total[rows * k : rows * (k + 1)].astype(out.dtype)
        out[k, rows:] = spare[...].astype(out.dtype)


def far_chunks(row_inv, col_inv, far, rows_right, cols_left):
    rows, half = far.shape[1], cols_left.shape[1]
    vmem = pl.BlockSpec(memory_space=pltpu.VMEM)
    chunk = jax.ShapeDtypeStruct((rows, half), jnp.bfloat16)
    return pl.pallas_call(
        far_kernel,
        out_shape=(
            chunk,
            chunk,
            jax.ShapeDtypeStruct((rows, 4 * rows), jnp.bfloat16),
            jax.ShapeDtypeStruct((4 * rows, rows), jnp.bfloat16),
        ),
        in_specs=[vmem] * 5,
        out_specs=(vmem,) * 4,
        compiler_params=pltpu.CompilerParams(vmem_limit_bytes=48 << 20),
        cost_estimate=pl.CostEstimate(
            flops=16 * rows * rows * half, transcendentals=0, bytes_accessed=8 << 20
        ),
        name="far_weights",
    )(row_inv, col_inv, far, rows_right, cols_left)


def call(kernel, name, flops, inputs, out_shape, scratch=(), scalars=0):
    vmem = pl.BlockSpec(memory_space=pltpu.VMEM)
    smem = pl.BlockSpec(memory_space=pltpu.SMEM)
    many = isinstance(out_shape, tuple)
    return pl.pallas_call(
        kernel,
        out_shape=out_shape,
        in_specs=[smem] * scalars + [vmem] * (len(inputs) - scalars),
        out_specs=(vmem,) * len(out_shape) if many else vmem,
        scratch_shapes=scratch,
        compiler_params=pltpu.CompilerParams(vmem_limit_bytes=48 << 20),
        cost_estimate=pl.CostEstimate(flops=flops, transcendentals=0, bytes_accessed=12 << 20),
        name=name,
    )(*inputs)


def per_device(hidden, projection, inv_temp, partners, positives):
    rows = hidden.shape[0]
    width = projection.shape[1]
    half = width // 2
    iy, ic = lax.axis_index("y"), lax.axis_index("core")
    iz, ix = lax.axis_index("z"), lax.axis_index("x")
    mine = iz * 4 + ix

    offsets = (partners[0] % 16) ^ mine
    back = jnp.arange(4)
    row_ids = iz * 4 + (ix - back) % 4
    col_ids = ((iz - back) % 4) * 4 + ix
    apart = (row_ids[:, None] ^ col_ids[None, :]).reshape(16)
    active = (jnp.any(apart[:, None] == offsets[None, :], axis=1) | (apart == 0)).astype(jnp.int32)
    pos = (positives % rows)[:, None]

    projected = jnp.dot(hidden, projection, preferred_element_type=jnp.float32)
    lengths = jnp.sqrt(jnp.sum(projected * projected, axis=1, keepdims=True) + epsilon)
    unit_rows = projected / lengths
    unit_low = unit_rows.astype(jnp.bfloat16)

    x_back, x_far, x_ahead = ring_gather(unit_low, "x")
    z_back, z_far, z_ahead = ring_gather(unit_low, "z")

    fourth = hidden.shape[1] // 4
    by_y = jnp.stack([hidden[:, fourth * k : fourth * (k + 1)] for k in range(4)])
    own_hidden = lax.all_to_all(by_y, "y", 0, 0)

    own = (unit_low,)
    near, near_rows, near_cols, hits = score_tiles(
        NEAR, False, active, inv_temp, pos, {0: own, 1: x_back, 3: x_ahead}, {0: own, 1: z_back, 3: z_ahead}
    )
    far, far_rows, far_cols, rows_right, cols_left = score_tiles(
        FAR,
        True,
        active,
        inv_temp,
        pos,
        {0: own, 1: x_back, 2: x_far, 3: x_ahead},
        {0: own, 1: z_back, 2: z_far, 3: z_ahead},
    )

    row_sums = jnp.sum(near_rows + far_rows, axis=2)
    hit_sum = jnp.full((4, 128), jnp.sum(hits)) * (back == 0)[:, None]
    row_totals = ring_total(jnp.concatenate([row_sums, hit_sum], axis=1), "x")
    row_totals, hit_sum = row_totals[:, :rows], row_totals[:, rows]
    col_totals = ring_total(jnp.sum(near_cols + far_cols, axis=1), "z")
    row_inv = jnp.broadcast_to((1.0 / row_totals)[:, :, None], (4, rows, 128))
    col_inv = (1.0 / col_totals)[:, None, :]
    row_inv, col_inv, own_hidden = lax.optimization_barrier((row_inv, col_inv, own_hidden))
    other_hidden = swap(own_hidden)

    far_row, far_col, wide, tall = far_chunks(row_inv, col_inv, far, rows_right, cols_left)
    cut = rows // 2
    seen = (
        send(far_row[:cut], "x", -1),
        send(far_row[cut:], "x", 1),
        send(far_col[:cut], "z", -1),
        send(far_col[cut:], "z", 1),
    )
    unit = 2 * rows * rows * half
    chunk = jax.ShapeDtypeStruct((rows, half), jnp.float32)
    low_chunk = jax.ShapeDtypeStruct((rows, half), jnp.bfloat16)
    square = jax.ShapeDtypeStruct((4 * rows, 4 * rows), jnp.bfloat16)
    by_row, by_col, weights = call(
        own_kernel, "own_weights", 8 * unit,
        (pos, row_inv, col_inv, near, wide, tall, rows_right, cols_left),
        (chunk, chunk, square),
    )
    x_next, x_last, z_next, z_last = call(
        near_kernel, "near_weights", 16 * unit,
        (weights, rows_right, cols_left, *seen),
        (low_chunk,) * 4,
    )
    x_sum = by_row + send(x_next, "x", -1).astype(jnp.float32) + send(x_last, "x", 1).astype(jnp.float32)
    z_sum = by_col + send(z_next, "z", -1).astype(jnp.float32) + send(z_last, "z", 1).astype(jnp.float32)
    halves = [x_sum, z_sum]
    halves, other_hidden = lax.optimization_barrier((halves, other_hidden))
    grad_unit = inv_temp[0] * jnp.concatenate(halves, axis=1)
    along = jnp.sum(unit_rows * grad_unit, axis=1, keepdims=True)
    grad_projected = ((grad_unit - unit_rows * along) / lengths).astype(jnp.bfloat16)
    grad_hidden = lax.dot_general(
        grad_projected, projection, (((1,), (1,)), ((), ())), preferred_element_type=jnp.float32
    ).astype(jnp.bfloat16)

    ring_loss = jnp.sum(shift + jnp.log(row_totals)) - jnp.sum(hit_sum)
    total = total_over_y(jnp.full((8, 128), ring_loss))

    left, right = grad_projected[:, :half], grad_projected[:, half:]
    kept = jnp.where(ic == 0, left, right)
    other = swap(jnp.where(ic == 0, right, left))
    own_back, other_back = send(kept, "y", 1), send(other, "y", 1)
    own_ahead, other_ahead = send(kept, "y", -1), send(other, "y", -1)
    own_far, other_far = send(own_back, "y", 1), send(other_ahead, "y", -1)
    places = (iy - back) % 4
    step = 2 * rows * fourth * half
    first = call(
        functools.partial(gather_kernel, (0, 1, 3)), "near_rows", 6 * step,
        (places, own_hidden, other_hidden, kept, own_back, own_ahead, other, other_back, other_ahead),
        jax.ShapeDtypeStruct((fourth, half), jnp.float32),
        scalars=1,
    )
    first, own_far, other_far, grad_hidden, total = lax.optimization_barrier(
        (first, own_far, other_far, grad_hidden, total)
    )
    high = lax.reduce_precision(total[0, 0], 8, 7)
    middle = lax.reduce_precision(total[0, 0] - high, 8, 7)
    low = total[0, 0] - high - middle
    spare = jnp.stack([high, middle, low, jnp.zeros_like(low)])
    part = call(
        last_kernel, "last_rows", 2 * step,
        (places, own_hidden, other_hidden, own_far, other_far, first, jnp.broadcast_to(spare[:, None], (4, half))),
        jax.ShapeDtypeStruct((32, fourth // 32 + 4, half), jnp.bfloat16),
        scratch=[pltpu.VMEM((fourth, half), jnp.float32)],
        scalars=1,
    )
    arrived = lax.all_to_all(part, ("core", "z", "x"), 0, 0).astype(jnp.float32)
    sums = jnp.sum(arrived.reshape(2, 16, fourth // 32 + 4, half), axis=1)
    grad_proj = jnp.concatenate([sums[0, : fourth // 32], sums[1, : fourth // 32]], axis=1)
    loss = jnp.sum(sums[:, fourth // 32 :, 0]) / (4 * 128 * rows)
    return (loss, grad_hidden, grad_proj)


def solution(mesh):
    split = Mesh(mesh.devices.reshape(4, 2, 4, 4), AXES)
    return jax.shard_map(
        per_device,
        mesh=split,
        in_specs=(P(AXES, None), P(), P(), P(AXES, None), P(AXES)),
        out_specs=(P(), P(AXES, None), P(AXES, None)),
        check_vma=False,
    )
```

```python
import functools

import jax
import jax.numpy as jnp
from jax import lax
from jax.experimental import pallas as pl
from jax.experimental.pallas import tpu as pltpu
from jax.sharding import Mesh, PartitionSpec as P

epsilon = 1e-06
shift = 3.0
AXES = ("y", "core", "z", "x")
ORDER = (0, 1, 3, 2)
NEAR = [(0, 0), (0, 1), (0, 3), (1, 0), (1, 1), (1, 3), (3, 0), (3, 1), (3, 3)]
FAR = [(0, 2), (1, 2), (3, 2), (2, 0), (2, 1), (2, 2), (2, 3)]


def send(array, axis, step):
    return lax.ppermute(array, axis, [(i, (i + step) % 4) for i in range(4)])


def swap(array):
    return lax.ppermute(array, "core", [(0, 1), (1, 0)])


def ring_gather(block, axis):
    half = block.shape[0] // 2
    back = send(block, axis, 1)
    ahead = send(block, axis, -1)
    far_top = send(back[:half], axis, 1)
    far_bottom = send(ahead[half:], axis, -1)
    return (back,), (far_top, far_bottom), (ahead,)


def ring_total(parts, axis):
    total = parts
    for d in (1, 2, 3):
        seen = send(parts, axis, -d)
        total = total + jnp.roll(seen, -d, axis=0)
    return total


def target_of(pos):
    rows = pos.shape[0]
    return lax.broadcasted_iota(jnp.int32, (rows, rows), 1) == pos


def score_kernel(tiles, names, pieces, final, *refs):
    active, scale, pos = refs[:3]
    count = sum(pieces)
    outs = refs[3 + 2 * count :]
    powers, row_sums, col_sums = outs[:3]
    rows = pos.shape[0]
    row_sums[...] = jnp.zeros_like(row_sums)
    col_sums[...] = jnp.zeros_like(col_sums)
    if final:
        outs[5][...] = jnp.zeros_like(outs[5])
    joined = list(outs[6:])
    row_units, col_units = [], []
    for refs_in, units in ((refs[3 : 3 + count], row_units), (refs[3 + count : 3 + 2 * count], col_units)):
        at = 0
        for many in pieces:
            source = refs_in[at]
            if many > 1:
                source = joined.pop()
                cut = rows // many
                for part in range(many):
                    source[cut * part : cut * (part + 1)] = refs_in[at + part][...]
            units.append(source)
            at += many
    factor = scale[0]
    for place, (dx, dz) in enumerate(tiles):
        scores = factor * lax.dot_general(
            row_units[names.index(dx)][...],
            col_units[names.index(dz)][...],
            (((1,), (1,)), ((), ())),
            preferred_element_type=jnp.float32,
        )
        power = jnp.exp(scores - shift)
        if (dx, dz) == (0, 0):
            here = lax.broadcasted_iota(jnp.int32, (rows, rows), 0)
            there = lax.broadcasted_iota(jnp.int32, (rows, rows), 1)
            power = jnp.where(here == there, 0.0, power)
            hit = jnp.where(target_of(pos[...]), scores, 0.0)
            outs[5][...] = hit[:, :128] + hit[:, 128:256] + hit[:, 256:]
        else:
            power = power * active[4 * dx + dz]
        powers[place] = power.astype(jnp.bfloat16)
        row_sums[dx] += power[:, :128] + power[:, 128:256] + power[:, 256:]
        col_sums[dz] += jnp.sum(power.reshape(rows // 8, 8, rows), axis=0)
    half = row_units[0].shape[1] // 2
    for place, d in enumerate([2] if final else names):
        outs[3][rows * place : rows * (place + 1)] = row_units[names.index(d)][:, half:]
        outs[4][rows * place : rows * (place + 1)] = col_units[names.index(d)][:, :half]


def score_tiles(tiles, final, active, scale, pos, row_pieces, col_pieces):
    names = sorted({d for tile in tiles for d in tile})
    rows = pos.shape[0]
    width = row_pieces[0][0].shape[1]
    smem = pl.BlockSpec(memory_space=pltpu.SMEM)
    vmem = pl.BlockSpec(memory_space=pltpu.VMEM)
    out_shape = [
        jax.ShapeDtypeStruct((len(tiles), rows, rows), jnp.bfloat16),
        jax.ShapeDtypeStruct((4, rows, 128), jnp.float32),
        jax.ShapeDtypeStruct((4, 8, rows), jnp.float32),
    ]
    out_shape += [jax.ShapeDtypeStruct(((1 if final else 3) * rows, width // 2), jnp.bfloat16)] * 2
    out_shape += [jax.ShapeDtypeStruct((8 if final else rows, 128), jnp.float32)]
    scratch = [pltpu.VMEM((rows, width), jnp.bfloat16)] * 2 if final else []
    pieces = [len(row_pieces[d]) for d in names]
    return pl.pallas_call(
        functools.partial(score_kernel, tiles, names, pieces, final),
        out_shape=tuple(out_shape),
        in_specs=[smem, smem] + [vmem] * (1 + 2 * sum(pieces)),
        out_specs=(vmem,) * len(out_shape),
        scratch_shapes=scratch,
        compiler_params=pltpu.CompilerParams(vmem_limit_bytes=48 << 20),
        cost_estimate=pl.CostEstimate(
            flops=len(tiles) * 2 * rows * rows * width,
            transcendentals=len(tiles) * rows * rows,
            bytes_accessed=16 << 20,
        ),
        name="scores",
    )(
        active, scale, pos,
        *[piece for d in names for piece in row_pieces[d]],
        *[piece for d in names for piece in col_pieces[d]],
    )


def weight_tile(source, place, dx, dz, row_inv, col_inv):
    inv = row_inv[dx]
    return source[place].astype(jnp.float32) * (jnp.concatenate([inv, inv, inv], axis=1) + col_inv[dz])


def product(left, right):
    return jnp.dot(left, right, preferred_element_type=jnp.float32)


def product_over_rows(left, right):
    return lax.dot_general(left, right, (((0,), (0,)), ((), ())), preferred_element_type=jnp.float32)


def far_kernel(row_inv, col_inv, far, rows_near, rows_far, cols_near, cols_far, far_row, far_col, wide, tall):
    rows = far.shape[1]
    for place, (dx, dz) in enumerate(FAR):
        weight = weight_tile(far, place, dx, dz, row_inv, col_inv).astype(jnp.bfloat16)
        if dx == 2:
            at = rows * ORDER.index(dz)
            wide[:, at : at + rows] = weight
        if dz == 2:
            at = rows * ORDER.index(dx)
            tall[at : at + rows] = weight
    by_row = product(wide[:, : 3 * rows], cols_near[...]) + product(wide[:, 3 * rows :], cols_far[...])
    by_col = product_over_rows(tall[: 3 * rows], rows_near[...]) + product_over_rows(tall[3 * rows :], rows_far[...])
    far_row[...] = by_row.astype(far_row.dtype)
    far_col[...] = by_col.astype(far_col.dtype)


def both_ways(d, weights, wide, tall, rows_near, rows_far, cols_near, cols_far):
    rows = wide.shape[0]
    span = slice(rows * ORDER.index(d), rows * (ORDER.index(d) + 1))
    by_row = product(weights[span], cols_near[...]) + product(tall[span], cols_far[...])
    by_col = product_over_rows(weights[:, span], rows_near[...]) + product_over_rows(wide[:, span], rows_far[...])
    return by_row, by_col


def own_kernel(*refs):
    by_row, by_col = both_ways(0, *refs[:7])
    refs[9][...] = by_row + refs[7][...].astype(jnp.float32)
    refs[10][...] = by_col + refs[8][...].astype(jnp.float32)


def near_kernel(pos, row_inv, col_inv, near, wide, tall, *refs):
    units, outs, weights = refs[:4], refs[4:8], refs[8]
    rows = pos.shape[0]
    for place, (dx, dz) in enumerate(NEAR):
        weight = weight_tile(near, place, dx, dz, row_inv, col_inv)
        if (dx, dz) == (0, 0):
            weight = weight - jnp.where(target_of(pos[...]), 2.0, 0.0)
        row, col = rows * ORDER.index(dx), rows * ORDER.index(dz)
        weights[row : row + rows, col : col + rows] = weight.astype(jnp.bfloat16)
    for place, d in enumerate((1, 3)):
        by_row, by_col = both_ways(d, weights, wide, tall, *units)
        outs[place][...] = by_row.astype(outs[place].dtype)
        outs[2 + place][...] = by_col.astype(outs[2 + place].dtype)


def split_value(value):
    high = value.astype(jnp.bfloat16).astype(jnp.float32)
    middle = (value - high).astype(jnp.bfloat16).astype(jnp.float32)
    low = value - high - middle
    row = lax.broadcasted_iota(jnp.int32, value.shape, 0)
    parts = jnp.where(row == 0, high, jnp.where(row == 1, middle, jnp.where(row == 2, low, 0.0)))
    return parts.astype(jnp.bfloat16)


def row_kernel(scale, core, ring_loss, by_row, by_col, *refs):
    arrivals, (unit_rows, lengths, whole, kept, other) = refs[:4], refs[4:]
    rows, half = by_row.shape
    left, right = by_row[...], by_col[...]
    for seen in arrivals[:2]:
        left = left + seen[...].astype(jnp.float32)
    for seen in arrivals[2:]:
        right = right + seen[...].astype(jnp.float32)
    left, right = scale[0] * left, scale[0] * right
    unit_left, unit_right = unit_rows[:, :half], unit_rows[:, half:]
    along = jnp.sum(unit_left * left, axis=1, keepdims=True) + jnp.sum(unit_right * right, axis=1, keepdims=True)
    length = lengths[...]
    left = ((left - unit_left * along) / length).astype(jnp.bfloat16)
    right = ((right - unit_right * along) / length).astype(jnp.bfloat16)
    whole[:, :half], whole[:, half:] = left, right
    kept[rows:] = split_value(jnp.full((16, half), ring_loss[0], jnp.float32))

    @pl.when(core[0] == 0)
    def _():
        kept[:rows], other[...] = left, right

    @pl.when(core[0] == 1)
    def _():
        kept[:rows], other[...] = right, left


def hidden_kernel(rows, weights, out):
    out[...] = lax.dot_general(
        rows[...], weights[...], (((1,), (1,)), ((), ())), preferred_element_type=jnp.float32
    ).astype(out.dtype)


def hidden_grad(rows, projection, steps=7):
    count, width = rows.shape
    depth = projection.shape[0]
    block = depth // steps
    return pl.pallas_call(
        hidden_kernel,
        grid=(steps,),
        out_shape=jax.ShapeDtypeStruct((count, depth), jnp.bfloat16),
        in_specs=[
            pl.BlockSpec((count, width), lambda i: (0, 0)),
            pl.BlockSpec((block, width), lambda i: (i, 0)),
        ],
        out_specs=pl.BlockSpec((count, block), lambda i: (0, i)),
        compiler_params=pltpu.CompilerParams(vmem_limit_bytes=48 << 20),
        cost_estimate=pl.CostEstimate(
            flops=2 * count * width * depth, transcendentals=0, bytes_accessed=11 << 20
        ),
        name="hidden_grad",
    )(rows, projection)


def gather_kernel(places, hidden_own, hidden_other, *refs):
    pairs, out = refs[:3], refs[3]
    rows = hidden_own.shape[1]
    step = pl.program_id(0)
    for k in range(3):
        @pl.when(step == k)
        def _():
            made = product_over_rows(hidden_own[0], pairs[k][:rows])
            made = made + product_over_rows(hidden_other[0], pairs[k][rows + 16 :])
            if k == 0:
                out[...] = made
            else:
                out[...] += made


def last_kernel(places, hidden_own, hidden_other, own, other, pair, back, ahead, first, out, total):
    rows = other.shape[0]
    total[...] = (
        first[...]
        + product_over_rows(hidden_own[0], own[:rows])
        + product_over_rows(hidden_other[0], other[...])
    )
    loss = jnp.zeros((1, own.shape[1]), jnp.float32)
    for source in (own, pair, back, ahead):
        loss = loss + jnp.sum(source[rows : rows + 16].astype(jnp.float32), axis=0, keepdims=True)
    spare = split_value(jnp.broadcast_to(loss, (16, own.shape[1])))[:4]
    count, padded = out.shape[:2]
    size = padded - 4
    for k in range(count):
        out[k, :size] = total[size * k : size * (k + 1)].astype(out.dtype)
        out[k, size:] = spare


def call_by_place(kernel, name, flops, places, hidden_own, hidden_other, inputs, out_shape, scratch=()):
    block = pl.BlockSpec((1,) + hidden_own.shape[1:], lambda i, places: (places[i], 0, 0))
    def all_of(shape):
        return pl.BlockSpec(shape, lambda i, places: (0,) * len(shape))
    return pl.pallas_call(
        kernel,
        out_shape=out_shape,
        grid_spec=pltpu.PrefetchScalarGridSpec(
            num_scalar_prefetch=1,
            grid=places.shape,
            in_specs=[block, block] + [all_of(array.shape) for array in inputs],
            out_specs=all_of(out_shape.shape),
            scratch_shapes=scratch,
        ),
        compiler_params=pltpu.CompilerParams(vmem_limit_bytes=48 << 20),
        cost_estimate=pl.CostEstimate(flops=flops, transcendentals=0, bytes_accessed=8 << 20),
        name=name,
    )(places, hidden_own, hidden_other, *inputs)


def call(kernel, name, flops, inputs, out_shape, scratch=(), scalars=0):
    vmem = pl.BlockSpec(memory_space=pltpu.VMEM)
    smem = pl.BlockSpec(memory_space=pltpu.SMEM)
    many = isinstance(out_shape, tuple)
    return pl.pallas_call(
        kernel,
        out_shape=out_shape,
        in_specs=[smem] * scalars + [vmem] * (len(inputs) - scalars),
        out_specs=(vmem,) * len(out_shape) if many else vmem,
        scratch_shapes=scratch,
        compiler_params=pltpu.CompilerParams(vmem_limit_bytes=48 << 20),
        cost_estimate=pl.CostEstimate(flops=flops, transcendentals=0, bytes_accessed=12 << 20),
        name=name,
    )(*inputs)


def per_device(hidden, projection, inv_temp, partners, positives):
    rows = hidden.shape[0]
    width = projection.shape[1]
    half = width // 2
    iy, ic = lax.axis_index("y"), lax.axis_index("core")
    iz, ix = lax.axis_index("z"), lax.axis_index("x")
    mine = iz * 4 + ix

    offsets = (partners[0] % 16) ^ mine
    back = jnp.arange(4)
    row_ids = iz * 4 + (ix - back) % 4
    col_ids = ((iz - back) % 4) * 4 + ix
    apart = (row_ids[:, None] ^ col_ids[None, :]).reshape(16)
    active = (jnp.any(apart[:, None] == offsets[None, :], axis=1) | (apart == 0)).astype(jnp.int32)
    pos = (positives % rows)[:, None]

    projected = jnp.dot(hidden, projection, preferred_element_type=jnp.float32)
    lengths = jnp.sqrt(jnp.sum(projected * projected, axis=1, keepdims=True) + epsilon)
    unit_rows = projected / lengths
    unit_low = unit_rows.astype(jnp.bfloat16)

    x_back, x_far, x_ahead = ring_gather(unit_low, "x")
    z_back, z_far, z_ahead = ring_gather(unit_low, "z")

    fourth = hidden.shape[1] // 4
    by_y = jnp.stack([hidden[:, fourth * k : fourth * (k + 1)] for k in range(4)])
    own_hidden = lax.all_to_all(by_y, "y", 0, 0)

    own = (unit_low,)
    near, near_rows, near_cols, rows_near, cols_near, hits = score_tiles(
        NEAR, False, active, inv_temp, pos, {0: own, 1: x_back, 3: x_ahead}, {0: own, 1: z_back, 3: z_ahead}
    )
    far, far_rows, far_cols, rows_far, cols_far, _ = score_tiles(
        FAR,
        True,
        active,
        inv_temp,
        pos,
        {0: own, 1: x_back, 2: x_far, 3: x_ahead},
        {0: own, 1: z_back, 2: z_far, 3: z_ahead},
    )

    row_sums = jnp.sum(near_rows + far_rows, axis=2)
    hit_sum = jnp.full((4, 128), jnp.sum(hits)) * (back == 0)[:, None]
    row_totals = ring_total(jnp.concatenate([row_sums, hit_sum], axis=1), "x")
    row_totals, hit_sum = row_totals[:, :rows], row_totals[:, rows]
    col_totals = ring_total(jnp.sum(near_cols + far_cols, axis=1), "z")
    row_inv = jnp.broadcast_to((1.0 / row_totals)[:, :, None], (4, rows, 128))
    col_inv = (1.0 / col_totals)[:, None, :]
    row_inv, col_inv, own_hidden = lax.optimization_barrier((row_inv, col_inv, own_hidden))
    other_hidden = swap(own_hidden)

    unit = 2 * rows * rows * half
    chunk = jax.ShapeDtypeStruct((rows, half), jnp.float32)
    low_chunk = jax.ShapeDtypeStruct((rows, half), jnp.bfloat16)
    units = (rows_near, rows_far, cols_near, cols_far)
    far_row, far_col, wide, tall = call(
        far_kernel, "far_weights", 8 * unit, (row_inv, col_inv, far, *units),
        (
            low_chunk,
            low_chunk,
            jax.ShapeDtypeStruct((rows, 4 * rows), jnp.bfloat16),
            jax.ShapeDtypeStruct((4 * rows, rows), jnp.bfloat16),
        ),
    )
    x_far_seen, z_far_seen = send(far_row, "x", 2), send(far_col, "z", 2)
    x_next, x_last, z_next, z_last, weights = call(
        near_kernel, "near_weights", 24 * unit, (pos, row_inv, col_inv, near, wide, tall, *units),
        (low_chunk,) * 4 + (jax.ShapeDtypeStruct((3 * rows, 3 * rows), jnp.bfloat16),),
    )
    arrivals = (send(x_next, "x", -1), send(x_last, "x", 1), send(z_next, "z", -1), send(z_last, "z", 1))
    by_row, by_col = call(own_kernel, "own_weights", 8 * unit, (weights, wide, tall, *units, x_far_seen, z_far_seen), (chunk, chunk))
    ring_loss = jnp.sum(shift + jnp.log(row_totals)) - jnp.sum(hit_sum)
    arrivals, other_hidden, ring_loss = lax.optimization_barrier((arrivals, other_hidden, ring_loss))
    grad_projected, kept, other = call(
        row_kernel, "row_gradients", unit,
        (inv_temp, ic[None], ring_loss[None], by_row, by_col, *arrivals, unit_rows, lengths),
        (
            jax.ShapeDtypeStruct((rows, width), jnp.bfloat16),
            jax.ShapeDtypeStruct((rows + 16, half), jnp.bfloat16),
            low_chunk,
        ),
        scalars=3,
    )
    pair = jnp.concatenate([kept, swap(other)], axis=0)
    grad_hidden = hidden_grad(grad_projected, projection)
    pair_back, pair_ahead = send(pair, "y", 1), send(pair, "y", -1)
    own_far = send(pair_back[: rows + 16], "y", 1)
    other_far = send(pair_ahead[rows + 16 :], "y", -1)
    step = 2 * rows * fourth * half
    first = call_by_place(
        gather_kernel, "near_rows", 60 * step, jnp.stack([iy, (iy + 3) % 4, (iy + 1) % 4]),
        own_hidden, other_hidden, (pair, pair_back, pair_ahead),
        jax.ShapeDtypeStruct((fourth, half), jnp.float32),
    )
    first, own_far, other_far, grad_hidden = lax.optimization_barrier((first, own_far, other_far, grad_hidden))
    part = call_by_place(
        last_kernel, "last_rows", 2 * step, ((iy + 2) % 4)[None], own_hidden, other_hidden,
        (own_far, other_far, pair, pair_back, pair_ahead, first),
        jax.ShapeDtypeStruct((32, fourth // 32 + 4, half), jnp.bfloat16),
        scratch=[pltpu.VMEM((fourth, half), jnp.float32)],
    )
    arrived = lax.all_to_all(part, ("core", "z", "x"), 0, 0).astype(jnp.float32)
    sums = jnp.sum(arrived.reshape(2, 16, fourth // 32 + 4, half), axis=1)
    grad_proj = jnp.concatenate([sums[0, : fourth // 32], sums[1, : fourth // 32]], axis=1)
    loss = jnp.sum(sums[:, fourth // 32 :, 0]) / (4 * 128 * rows)
    return (loss, grad_hidden, grad_proj)


def solution(mesh):
    split = Mesh(mesh.devices.reshape(4, 2, 4, 4), AXES)
    return jax.shard_map(
        per_device,
        mesh=split,
        in_specs=(P(AXES, None), P(), P(), P(AXES, None), P(AXES)),
        out_specs=(P(), P(AXES, None), P(AXES, None)),
        check_vma=False,
    )
```

```python
import functools

import jax
import jax.numpy as jnp
from jax import lax
from jax.experimental import pallas as pl
from jax.experimental.pallas import tpu as pltpu
from jax.sharding import Mesh, PartitionSpec as P

epsilon = 1e-06
shift = 3.0
AXES = ("y", "core", "z", "x")
ORDER = (0, 1, 3, 2)
NEAR = [(0, 0), (0, 1), (0, 3), (1, 0), (1, 1), (1, 3), (3, 0), (3, 1), (3, 3)]
FAR = [(0, 2), (1, 2), (3, 2), (2, 0), (2, 1), (2, 2), (2, 3)]


def send(array, axis, step):
    pairs = [(core, i, (i + (1 - 2 * core) * step) % 4) for core in range(2) for i in range(4)]
    if axis == "y":
        return lax.ppermute(array, ("y", "core"), [(2 * i + core, 2 * j + core) for core, i, j in pairs])
    return lax.ppermute(array, ("core", axis), [(4 * core + i, 4 * core + j) for core, i, j in pairs])


def swap(array):
    return lax.ppermute(array, "core", [(0, 1), (1, 0)])


def ring_gather(block, axis):
    back = send(block, axis, 1)
    ahead = send(block, axis, -1)
    return (back,), (send(back, axis, 1),), (ahead,)


def ring_total(parts, axis):
    total = parts
    for d in (1, 2, 3):
        seen = send(parts, axis, -d)
        total = total + jnp.roll(seen, -d, axis=0)
    return total


def target_of(pos):
    rows = pos.shape[0]
    return lax.broadcasted_iota(jnp.int32, (rows, rows), 1) == pos


def score_kernel(tiles, names, pieces, final, *refs):
    active, scale, pos = refs[:3]
    count = sum(pieces)
    outs = refs[3 + 2 * count :]
    powers, row_sums, col_sums = outs[:3]
    rows = pos.shape[0]
    row_sums[...] = jnp.zeros_like(row_sums)
    col_sums[...] = jnp.zeros_like(col_sums)
    if final:
        outs[5][...] = jnp.zeros_like(outs[5])
    joined = list(outs[6:])
    row_units, col_units = [], []
    for refs_in, units in ((refs[3 : 3 + count], row_units), (refs[3 + count : 3 + 2 * count], col_units)):
        at = 0
        for many in pieces:
            source = refs_in[at]
            if many > 1:
                source = joined.pop()
                cut = rows // many
                for part in range(many):
                    source[cut * part : cut * (part + 1)] = refs_in[at + part][...]
            units.append(source)
            at += many
    factor = scale[0]
    for place, (dx, dz) in enumerate(tiles):
        scores = factor * lax.dot_general(
            row_units[names.index(dx)][...],
            col_units[names.index(dz)][...],
            (((1,), (1,)), ((), ())),
            preferred_element_type=jnp.float32,
        )
        power = jnp.exp(scores - shift)
        if (dx, dz) == (0, 0):
            here = lax.broadcasted_iota(jnp.int32, (rows, rows), 0)
            there = lax.broadcasted_iota(jnp.int32, (rows, rows), 1)
            power = jnp.where(here == there, 0.0, power)
            hit = jnp.where(target_of(pos[...]), scores, 0.0)
            outs[5][...] = hit[:, :128] + hit[:, 128:256] + hit[:, 256:]
        else:
            power = power * active[4 * dx + dz]
        powers[place] = power.astype(jnp.bfloat16)
        row_sums[dx] += power[:, :128] + power[:, 128:256] + power[:, 256:]
        col_sums[dz] += jnp.sum(power.reshape(rows // 8, 8, rows), axis=0)
    half = row_units[0].shape[1] // 2
    for place, d in enumerate([2] if final else names):
        outs[3][rows * place : rows * (place + 1)] = row_units[names.index(d)][:, half:]
        outs[4][rows * place : rows * (place + 1)] = col_units[names.index(d)][:, :half]


def score_tiles(tiles, final, active, scale, pos, row_pieces, col_pieces):
    names = sorted({d for tile in tiles for d in tile})
    rows = pos.shape[0]
    width = row_pieces[0][0].shape[1]
    smem = pl.BlockSpec(memory_space=pltpu.SMEM)
    vmem = pl.BlockSpec(memory_space=pltpu.VMEM)
    out_shape = [
        jax.ShapeDtypeStruct((len(tiles), rows, rows), jnp.bfloat16),
        jax.ShapeDtypeStruct((4, rows, 128), jnp.float32),
        jax.ShapeDtypeStruct((4, 8, rows), jnp.float32),
    ]
    out_shape += [jax.ShapeDtypeStruct(((1 if final else 3) * rows, width // 2), jnp.bfloat16)] * 2
    out_shape += [jax.ShapeDtypeStruct((8 if final else rows, 128), jnp.float32)]
    scratch = []
    pieces = [len(row_pieces[d]) for d in names]
    return pl.pallas_call(
        functools.partial(score_kernel, tiles, names, pieces, final),
        out_shape=tuple(out_shape),
        in_specs=[smem, smem] + [vmem] * (1 + 2 * sum(pieces)),
        out_specs=(vmem,) * len(out_shape),
        scratch_shapes=scratch,
        compiler_params=pltpu.CompilerParams(vmem_limit_bytes=48 << 20),
        cost_estimate=pl.CostEstimate(
            flops=len(tiles) * 2 * rows * rows * width,
            transcendentals=len(tiles) * rows * rows,
            bytes_accessed=16 << 20,
        ),
        name="scores",
    )(
        active, scale, pos,
        *[piece for d in names for piece in row_pieces[d]],
        *[piece for d in names for piece in col_pieces[d]],
    )


def weight_tile(source, place, dx, dz, row_inv, col_inv):
    inv = row_inv[dx]
    return source[place].astype(jnp.float32) * (jnp.concatenate([inv, inv, inv], axis=1) + col_inv[dz])


def product(left, right):
    return jnp.dot(left, right, preferred_element_type=jnp.float32)


def product_over_rows(left, right):
    return lax.dot_general(left, right, (((0,), (0,)), ((), ())), preferred_element_type=jnp.float32)


def far_kernel(row_inv, col_inv, far, rows_near, rows_far, cols_near, cols_far, far_row, far_col, wide, tall):
    rows = far.shape[1]
    for place, (dx, dz) in enumerate(FAR):
        weight = weight_tile(far, place, dx, dz, row_inv, col_inv).astype(jnp.bfloat16)
        if dx == 2:
            at = rows * ORDER.index(dz)
            wide[:, at : at + rows] = weight
        if dz == 2:
            at = rows * ORDER.index(dx)
            tall[at : at + rows] = weight
    by_row = product(wide[:, : 3 * rows], cols_near[...]) + product(wide[:, 3 * rows :], cols_far[...])
    by_col = product_over_rows(tall[: 3 * rows], rows_near[...]) + product_over_rows(tall[3 * rows :], rows_far[...])
    far_row[...] = by_row.astype(far_row.dtype)
    far_col[...] = by_col.astype(far_col.dtype)


def both_ways(d, weights, wide, tall, rows_near, rows_far, cols_near, cols_far):
    rows = wide.shape[0]
    span = slice(rows * ORDER.index(d), rows * (ORDER.index(d) + 1))
    by_row = product(weights[span], cols_near[...]) + product(tall[span], cols_far[...])
    by_col = product_over_rows(weights[:, span], rows_near[...]) + product_over_rows(wide[:, span], rows_far[...])
    return by_row, by_col


def own_kernel(*refs):
    by_row, by_col = both_ways(0, *refs[:7])
    refs[9][...] = by_row + refs[7][...].astype(jnp.float32)
    refs[10][...] = by_col + refs[8][...].astype(jnp.float32)


def near_kernel(pos, row_inv, col_inv, near, wide, tall, *refs):
    units, outs, weights = refs[:4], refs[4:8], refs[8]
    rows = pos.shape[0]
    for place, (dx, dz) in enumerate(NEAR):
        weight = weight_tile(near, place, dx, dz, row_inv, col_inv)
        if (dx, dz) == (0, 0):
            weight = weight - jnp.where(target_of(pos[...]), 2.0, 0.0)
        row, col = rows * ORDER.index(dx), rows * ORDER.index(dz)
        weights[row : row + rows, col : col + rows] = weight.astype(jnp.bfloat16)
    for place, d in enumerate((1, 3)):
        by_row, by_col = both_ways(d, weights, wide, tall, *units)
        outs[place][...] = by_row.astype(outs[place].dtype)
        outs[2 + place][...] = by_col.astype(outs[2 + place].dtype)


def split_value(value):
    high = value.astype(jnp.bfloat16).astype(jnp.float32)
    middle = (value - high).astype(jnp.bfloat16).astype(jnp.float32)
    low = value - high - middle
    row = lax.broadcasted_iota(jnp.int32, value.shape, 0)
    parts = jnp.where(row == 0, high, jnp.where(row == 1, middle, jnp.where(row == 2, low, 0.0)))
    return parts.astype(jnp.bfloat16)


def row_kernel(scale, core, ring_loss, by_row, by_col, *refs):
    arrivals, (unit_rows, lengths, whole, kept, other) = refs[:4], refs[4:]
    rows, half = by_row.shape
    left, right = by_row[...], by_col[...]
    for seen in arrivals[:2]:
        left = left + seen[...].astype(jnp.float32)
    for seen in arrivals[2:]:
        right = right + seen[...].astype(jnp.float32)
    left, right = scale[0] * left, scale[0] * right
    unit_left, unit_right = unit_rows[:, :half], unit_rows[:, half:]
    along = jnp.sum(unit_left * left, axis=1, keepdims=True) + jnp.sum(unit_right * right, axis=1, keepdims=True)
    length = lengths[...]
    left = ((left - unit_left * along) / length).astype(jnp.bfloat16)
    right = ((right - unit_right * along) / length).astype(jnp.bfloat16)
    whole[:, :half], whole[:, half:] = left, right
    kept[rows:] = split_value(jnp.full((16, half), ring_loss[0], jnp.float32))

    @pl.when(core[0] == 0)
    def _():
        kept[:rows], other[...] = left, right

    @pl.when(core[0] == 1)
    def _():
        kept[:rows], other[...] = right, left


def hidden_kernel(rows, weights, out):
    out[...] = lax.dot_general(
        rows[...], weights[...], (((1,), (1,)), ((), ())), preferred_element_type=jnp.float32
    ).astype(out.dtype)


def hidden_grad(rows, projection, steps=7):
    count, width = rows.shape
    depth = projection.shape[0]
    block = depth // steps
    return pl.pallas_call(
        hidden_kernel,
        grid=(steps,),
        out_shape=jax.ShapeDtypeStruct((count, depth), jnp.bfloat16),
        in_specs=[
            pl.BlockSpec((count, width), lambda i: (0, 0)),
            pl.BlockSpec((block, width), lambda i: (i, 0)),
        ],
        out_specs=pl.BlockSpec((count, block), lambda i: (0, i)),
        compiler_params=pltpu.CompilerParams(vmem_limit_bytes=48 << 20),
        cost_estimate=pl.CostEstimate(
            flops=2 * count * width * depth, transcendentals=0, bytes_accessed=11 << 20
        ),
        name="hidden_grad",
    )(rows, projection)


def gather_kernel(places, hidden_own, hidden_other, *refs):
    own, other, out = refs[:3], refs[3:6], refs[6]
    rows = hidden_own.shape[1]
    step = pl.program_id(0)
    for k in range(3):
        @pl.when(step == k)
        def _():
            made = product_over_rows(hidden_own[0], own[k][:rows])
            made = made + product_over_rows(hidden_other[0], other[k][...])
            if k == 0:
                out[...] = made
            else:
                out[...] += made


def last_kernel(places, hidden_own, hidden_other, far, other_far, kept, back, ahead, first, out, total):
    rows = hidden_own.shape[1]
    total[...] = (
        first[...]
        + product_over_rows(hidden_own[0], far[:rows])
        + product_over_rows(hidden_other[0], other_far[...])
    )
    loss = jnp.zeros((1, far.shape[1]), jnp.float32)
    for source in (far, kept, back, ahead):
        loss = loss + jnp.sum(source[rows : rows + 16].astype(jnp.float32), axis=0, keepdims=True)
    spare = split_value(jnp.broadcast_to(loss, (16, far.shape[1])))[:4]
    count, padded = out.shape[:2]
    size = padded - 4
    for k in range(count):
        out[k, :size] = total[size * k : size * (k + 1)].astype(out.dtype)
        out[k, size:] = spare


def call_by_place(kernel, name, flops, places, hidden_own, hidden_other, inputs, out_shape, scratch=()):
    block = pl.BlockSpec((1,) + hidden_own.shape[1:], lambda i, places: (places[i], 0, 0))
    def all_of(shape):
        return pl.BlockSpec(shape, lambda i, places: (0,) * len(shape))
    return pl.pallas_call(
        kernel,
        out_shape=out_shape,
        grid_spec=pltpu.PrefetchScalarGridSpec(
            num_scalar_prefetch=1,
            grid=places.shape,
            in_specs=[block, block] + [all_of(array.shape) for array in inputs],
            out_specs=all_of(out_shape.shape),
            scratch_shapes=scratch,
        ),
        compiler_params=pltpu.CompilerParams(vmem_limit_bytes=48 << 20),
        cost_estimate=pl.CostEstimate(flops=flops, transcendentals=0, bytes_accessed=8 << 20),
        name=name,
    )(places, hidden_own, hidden_other, *inputs)


def call(kernel, name, flops, inputs, out_shape, scratch=(), scalars=0):
    vmem = pl.BlockSpec(memory_space=pltpu.VMEM)
    smem = pl.BlockSpec(memory_space=pltpu.SMEM)
    many = isinstance(out_shape, tuple)
    return pl.pallas_call(
        kernel,
        out_shape=out_shape,
        in_specs=[smem] * scalars + [vmem] * (len(inputs) - scalars),
        out_specs=(vmem,) * len(out_shape) if many else vmem,
        scratch_shapes=scratch,
        compiler_params=pltpu.CompilerParams(vmem_limit_bytes=48 << 20),
        cost_estimate=pl.CostEstimate(flops=flops, transcendentals=0, bytes_accessed=12 << 20),
        name=name,
    )(*inputs)


def per_device(hidden, projection, inv_temp, partners, positives):
    rows = hidden.shape[0]
    width = projection.shape[1]
    half = width // 2
    iy, ic = lax.axis_index("y"), lax.axis_index("core")
    iz, ix = lax.axis_index("z"), lax.axis_index("x")
    mine = iz * 4 + ix

    offsets = (partners[0] % 16) ^ mine
    back = jnp.arange(4)
    way = 1 - 2 * ic
    row_ids = iz * 4 + (ix - way * back) % 4
    col_ids = ((iz - way * back) % 4) * 4 + ix
    apart = (row_ids[:, None] ^ col_ids[None, :]).reshape(16)
    active = (jnp.any(apart[:, None] == offsets[None, :], axis=1) | (apart == 0)).astype(jnp.int32)
    pos = (positives % rows)[:, None]

    projected = jnp.dot(hidden, projection, preferred_element_type=jnp.float32)
    lengths = jnp.sqrt(jnp.sum(projected * projected, axis=1, keepdims=True) + epsilon)
    unit_rows = projected / lengths
    unit_low = unit_rows.astype(jnp.bfloat16)

    x_back, x_far, x_ahead = ring_gather(unit_low, "x")
    z_back, z_far, z_ahead = ring_gather(unit_low, "z")

    fourth = hidden.shape[1] // 4
    by_y = jnp.stack([hidden[:, fourth * k : fourth * (k + 1)] for k in range(4)])
    own_hidden = lax.all_to_all(by_y, "y", 0, 0)

    own = (unit_low,)
    near, near_rows, near_cols, rows_near, cols_near, hits = score_tiles(
        NEAR, False, active, inv_temp, pos, {0: own, 1: x_back, 3: x_ahead}, {0: own, 1: z_back, 3: z_ahead}
    )
    far, far_rows, far_cols, rows_far, cols_far, _ = score_tiles(
        FAR,
        True,
        active,
        inv_temp,
        pos,
        {0: own, 1: x_back, 2: x_far, 3: x_ahead},
        {0: own, 1: z_back, 2: z_far, 3: z_ahead},
    )

    row_sums = jnp.sum(near_rows + far_rows, axis=2)
    hit_sum = jnp.full((4, 128), jnp.sum(hits)) * (back == 0)[:, None]
    row_totals = ring_total(jnp.concatenate([row_sums, hit_sum], axis=1), "x")
    row_totals, hit_sum = row_totals[:, :rows], row_totals[:, rows]
    col_totals = ring_total(jnp.sum(near_cols + far_cols, axis=1), "z")
    row_inv = jnp.broadcast_to((1.0 / row_totals)[:, :, None], (4, rows, 128))
    col_inv = (1.0 / col_totals)[:, None, :]
    row_inv, col_inv, own_hidden = lax.optimization_barrier((row_inv, col_inv, own_hidden))
    other_hidden = swap(own_hidden)

    unit = 2 * rows * rows * half
    chunk = jax.ShapeDtypeStruct((rows, half), jnp.float32)
    low_chunk = jax.ShapeDtypeStruct((rows, half), jnp.bfloat16)
    units = (rows_near, rows_far, cols_near, cols_far)
    far_row, far_col, wide, tall = call(
        far_kernel, "far_weights", 8 * unit, (row_inv, col_inv, far, *units),
        (
            low_chunk,
            low_chunk,
            jax.ShapeDtypeStruct((rows, 4 * rows), jnp.bfloat16),
            jax.ShapeDtypeStruct((4 * rows, rows), jnp.bfloat16),
        ),
    )
    x_far_seen, z_far_seen = send(far_row, "x", 2), send(far_col, "z", 2)
    x_next, x_last, z_next, z_last, weights = call(
        near_kernel, "near_weights", 24 * unit, (pos, row_inv, col_inv, near, wide, tall, *units),
        (low_chunk,) * 4 + (jax.ShapeDtypeStruct((3 * rows, 3 * rows), jnp.bfloat16),),
    )
    arrivals = (send(x_next, "x", -1), send(x_last, "x", 1), send(z_next, "z", -1), send(z_last, "z", 1))
    by_row, by_col = call(own_kernel, "own_weights", 8 * unit, (weights, wide, tall, *units, x_far_seen, z_far_seen), (chunk, chunk))
    ring_loss = jnp.sum(shift + jnp.log(row_totals)) - jnp.sum(hit_sum)
    arrivals, other_hidden, ring_loss = lax.optimization_barrier((arrivals, other_hidden, ring_loss))
    grad_projected, kept, other = call(
        row_kernel, "row_gradients", unit,
        (inv_temp, ic[None], ring_loss[None], by_row, by_col, *arrivals, unit_rows, lengths),
        (
            jax.ShapeDtypeStruct((rows, width), jnp.bfloat16),
            jax.ShapeDtypeStruct((rows + 16, half), jnp.bfloat16),
            low_chunk,
        ),
        scalars=3,
    )
    own_back, own_ahead = send(kept, "y", 1), send(kept, "y", -1)
    other = swap(other)
    other_back, other_ahead = send(other, "y", 1), send(other, "y", -1)
    grad_hidden = hidden_grad(grad_projected, projection)
    own_far, other_far = send(own_back, "y", 1), send(other_back, "y", 1)
    step = 2 * rows * fourth * half
    first = call_by_place(
        gather_kernel, "near_rows", 60 * step, jnp.stack([iy, (iy - way) % 4, (iy + way) % 4]),
        own_hidden, other_hidden, (kept, own_back, own_ahead, other, other_back, other_ahead),
        jax.ShapeDtypeStruct((fourth, half), jnp.float32),
    )
    first, own_far, other_far, grad_hidden = lax.optimization_barrier((first, own_far, other_far, grad_hidden))
    part = call_by_place(
        last_kernel, "last_rows", 2 * step, ((iy + 2) % 4)[None], own_hidden, other_hidden,
        (own_far, other_far, kept, own_back, own_ahead, first),
        jax.ShapeDtypeStruct((32, fourth // 32 + 4, half), jnp.bfloat16),
        scratch=[pltpu.VMEM((fourth, half), jnp.float32)],
    )
    arrived = lax.all_to_all(part, ("core", "z", "x"), 0, 0).astype(jnp.float32)
    sums = jnp.sum(arrived.reshape(2, 16, fourth // 32 + 4, half), axis=1)
    grad_proj = jnp.concatenate([sums[0, : fourth // 32], sums[1, : fourth // 32]], axis=1)
    loss = jnp.sum(sums[:, fourth // 32 :, 0]) / (4 * 128 * rows)
    return (loss, grad_hidden, grad_proj)


def solution(mesh):
    split = Mesh(mesh.devices.reshape(4, 2, 4, 4), AXES)
    return jax.shard_map(
        per_device,
        mesh=split,
        in_specs=(P(AXES, None), P(), P(), P(AXES, None), P(AXES)),
        out_specs=(P(), P(AXES, None), P(AXES, None)),
        check_vma=False,
    )
```

```python
import functools

import jax
import jax.numpy as jnp
from jax import lax
from jax.experimental import pallas as pl
from jax.experimental.pallas import tpu as pltpu
from jax.sharding import Mesh, PartitionSpec as P

epsilon = 1e-06
shift = 3.0
AXES = ("y", "core", "z", "x")
ORDER = (0, 1, 3, 2)
NEAR = [(0, 0), (0, 1), (0, 3), (1, 0), (1, 1), (1, 3), (3, 0), (3, 1), (3, 3)]
FAR = [(0, 2), (1, 2), (3, 2), (2, 0), (2, 1), (2, 2), (2, 3)]


def send(array, axis, step):
    pairs = [(core, i, (i + (1 - 2 * core) * step) % 4) for core in range(2) for i in range(4)]
    if axis == "y":
        return lax.ppermute(array, ("y", "core"), [(2 * i + core, 2 * j + core) for core, i, j in pairs])
    return lax.ppermute(array, ("core", axis), [(4 * core + i, 4 * core + j) for core, i, j in pairs])


def swap(array):
    return lax.ppermute(array, "core", [(0, 1), (1, 0)])


def ring_gather(block, axis):
    back = send(block, axis, 1)
    ahead = send(block, axis, -1)
    return (back,), (send(back, axis, 1),), (ahead,)


def ring_total(parts, axis):
    total = parts
    for d in (1, 2, 3):
        seen = send(parts, axis, -d)
        total = total + jnp.roll(seen, -d, axis=0)
    return total


def target_of(pos):
    rows = pos.shape[0]
    return lax.broadcasted_iota(jnp.int32, (rows, rows), 1) == pos


def score_kernel(tiles, names, pieces, final, *refs):
    active, scale, pos = refs[:3]
    count = sum(pieces)
    outs = refs[3 + 2 * count :]
    powers, row_sums, col_sums = outs[:3]
    rows = pos.shape[0]
    row_sums[...] = jnp.zeros_like(row_sums)
    col_sums[...] = jnp.zeros_like(col_sums)
    if final:
        outs[5][...] = jnp.zeros_like(outs[5])
    joined = list(outs[6:])
    row_units, col_units = [], []
    for refs_in, units in ((refs[3 : 3 + count], row_units), (refs[3 + count : 3 + 2 * count], col_units)):
        at = 0
        for many in pieces:
            source = refs_in[at]
            if many > 1:
                source = joined.pop()
                cut = rows // many
                for part in range(many):
                    source[cut * part : cut * (part + 1)] = refs_in[at + part][...]
            units.append(source)
            at += many
    factor = scale[0]
    for place, (dx, dz) in enumerate(tiles):
        scores = factor * lax.dot_general(
            row_units[names.index(dx)][...],
            col_units[names.index(dz)][...],
            (((1,), (1,)), ((), ())),
            preferred_element_type=jnp.float32,
        )
        power = jnp.exp(scores - shift)
        if (dx, dz) == (0, 0):
            here = lax.broadcasted_iota(jnp.int32, (rows, rows), 0)
            there = lax.broadcasted_iota(jnp.int32, (rows, rows), 1)
            power = jnp.where(here == there, 0.0, power)
            hit = jnp.where(target_of(pos[...]), scores, 0.0)
            outs[5][...] = hit[:, :128] + hit[:, 128:256] + hit[:, 256:]
        else:
            power = power * active[4 * dx + dz]
        powers[place] = power.astype(jnp.bfloat16)
        row_sums[dx] += power[:, :128] + power[:, 128:256] + power[:, 256:]
        col_sums[dz] += jnp.sum(power.reshape(rows // 8, 8, rows), axis=0)
    half = row_units[0].shape[1] // 2
    for place, d in enumerate([2] if final else names):
        outs[3][rows * place : rows * (place + 1)] = row_units[names.index(d)][:, half:]
        outs[4][rows * place : rows * (place + 1)] = col_units[names.index(d)][:, :half]


def score_tiles(tiles, final, active, scale, pos, row_pieces, col_pieces):
    names = sorted({d for tile in tiles for d in tile})
    rows = pos.shape[0]
    width = row_pieces[0][0].shape[1]
    smem = pl.BlockSpec(memory_space=pltpu.SMEM)
    vmem = pl.BlockSpec(memory_space=pltpu.VMEM)
    out_shape = [
        jax.ShapeDtypeStruct((len(tiles), rows, rows), jnp.bfloat16),
        jax.ShapeDtypeStruct((4, rows, 128), jnp.float32),
        jax.ShapeDtypeStruct((4, 8, rows), jnp.float32),
    ]
    out_shape += [jax.ShapeDtypeStruct(((1 if final else 3) * rows, width // 2), jnp.bfloat16)] * 2
    out_shape += [jax.ShapeDtypeStruct((8 if final else rows, 128), jnp.float32)]
    scratch = []
    pieces = [len(row_pieces[d]) for d in names]
    return pl.pallas_call(
        functools.partial(score_kernel, tiles, names, pieces, final),
        out_shape=tuple(out_shape),
        in_specs=[smem, smem] + [vmem] * (1 + 2 * sum(pieces)),
        out_specs=(vmem,) * len(out_shape),
        scratch_shapes=scratch,
        compiler_params=pltpu.CompilerParams(vmem_limit_bytes=48 << 20),
        cost_estimate=pl.CostEstimate(
            flops=len(tiles) * 2 * rows * rows * width,
            transcendentals=len(tiles) * rows * rows,
            bytes_accessed=16 << 20,
        ),
        name="scores",
    )(
        active, scale, pos,
        *[piece for d in names for piece in row_pieces[d]],
        *[piece for d in names for piece in col_pieces[d]],
    )


def weight_tile(source, place, dx, dz, row_inv, col_inv):
    inv = row_inv[dx]
    return source[place].astype(jnp.float32) * (jnp.concatenate([inv, inv, inv], axis=1) + col_inv[dz])


def product(left, right):
    return jnp.dot(left, right, preferred_element_type=jnp.float32)


def product_over_rows(left, right):
    return lax.dot_general(left, right, (((0,), (0,)), ((), ())), preferred_element_type=jnp.float32)


def far_kernel(row_inv, col_inv, far, rows_near, rows_far, cols_near, cols_far, far_row, far_col, wide, tall):
    rows = far.shape[1]
    for place, (dx, dz) in enumerate(FAR):
        weight = weight_tile(far, place, dx, dz, row_inv, col_inv).astype(jnp.bfloat16)
        if dx == 2:
            at = rows * ORDER.index(dz)
            wide[:, at : at + rows] = weight
        if dz == 2:
            at = rows * ORDER.index(dx)
            tall[at : at + rows] = weight
    by_row = product(wide[:, : 3 * rows], cols_near[...]) + product(wide[:, 3 * rows :], cols_far[...])
    by_col = product_over_rows(tall[: 3 * rows], rows_near[...]) + product_over_rows(tall[3 * rows :], rows_far[...])
    far_row[...] = by_row.astype(far_row.dtype)
    far_col[...] = by_col.astype(far_col.dtype)


def both_ways(d, weights, wide, tall, rows_near, rows_far, cols_near, cols_far):
    rows = wide.shape[0]
    span = slice(rows * ORDER.index(d), rows * (ORDER.index(d) + 1))
    by_row = product(weights[span], cols_near[...]) + product(tall[span], cols_far[...])
    by_col = product_over_rows(weights[:, span], rows_near[...]) + product_over_rows(wide[:, span], rows_far[...])
    return by_row, by_col


def own_kernel(*refs):
    by_row, by_col = both_ways(0, *refs[:7])
    refs[9][...] = by_row + refs[7][...].astype(jnp.float32)
    refs[10][...] = by_col + refs[8][...].astype(jnp.float32)


def near_kernel(pos, row_inv, col_inv, near, wide, tall, *refs):
    units, outs, weights = refs[:4], refs[4:8], refs[8]
    rows = pos.shape[0]
    for place, (dx, dz) in enumerate(NEAR):
        weight = weight_tile(near, place, dx, dz, row_inv, col_inv)
        if (dx, dz) == (0, 0):
            weight = weight - jnp.where(target_of(pos[...]), 2.0, 0.0)
        row, col = rows * ORDER.index(dx), rows * ORDER.index(dz)
        weights[row : row + rows, col : col + rows] = weight.astype(jnp.bfloat16)
    for place, d in enumerate((1, 3)):
        by_row, by_col = both_ways(d, weights, wide, tall, *units)
        outs[place][...] = by_row.astype(outs[place].dtype)
        outs[2 + place][...] = by_col.astype(outs[2 + place].dtype)


def split_value(value):
    high = value.astype(jnp.bfloat16).astype(jnp.float32)
    middle = (value - high).astype(jnp.bfloat16).astype(jnp.float32)
    low = value - high - middle
    row = lax.broadcasted_iota(jnp.int32, value.shape, 0)
    parts = jnp.where(row == 0, high, jnp.where(row == 1, middle, jnp.where(row == 2, low, 0.0)))
    return parts.astype(jnp.bfloat16)


def row_kernel(scale, core, ring_loss, by_row, by_col, *refs):
    arrivals, (unit_rows, lengths, whole, kept, other) = refs[:4], refs[4:]
    rows, half = by_row.shape
    left, right = by_row[...], by_col[...]
    for seen in arrivals[:2]:
        left = left + seen[...].astype(jnp.float32)
    for seen in arrivals[2:]:
        right = right + seen[...].astype(jnp.float32)
    left, right = scale[0] * left, scale[0] * right
    unit_left, unit_right = unit_rows[:, :half], unit_rows[:, half:]
    along = jnp.sum(unit_left * left, axis=1, keepdims=True) + jnp.sum(unit_right * right, axis=1, keepdims=True)
    length = lengths[...]
    left = ((left - unit_left * along) / length).astype(jnp.bfloat16)
    right = ((right - unit_right * along) / length).astype(jnp.bfloat16)
    whole[:, :half], whole[:, half:] = left, right
    kept[rows:] = split_value(jnp.full((16, half), ring_loss[0], jnp.float32))

    @pl.when(core[0] == 0)
    def _():
        kept[:rows], other[...] = left, right

    @pl.when(core[0] == 1)
    def _():
        kept[:rows], other[...] = right, left


def hidden_kernel(rows, weights, out):
    out[...] = lax.dot_general(
        rows[...], weights[...], (((1,), (1,)), ((), ())), preferred_element_type=jnp.float32
    ).astype(out.dtype)


def hidden_grad(rows, projection, steps=7):
    count, width = rows.shape
    depth = projection.shape[0]
    block = depth // steps
    return pl.pallas_call(
        hidden_kernel,
        grid=(steps,),
        out_shape=jax.ShapeDtypeStruct((count, depth), jnp.bfloat16),
        in_specs=[
            pl.BlockSpec((count, width), lambda i: (0, 0)),
            pl.BlockSpec((block, width), lambda i: (i, 0)),
        ],
        out_specs=pl.BlockSpec((count, block), lambda i: (0, i)),
        compiler_params=pltpu.CompilerParams(vmem_limit_bytes=48 << 20),
        cost_estimate=pl.CostEstimate(
            flops=2 * count * width * depth, transcendentals=0, bytes_accessed=11 << 20
        ),
        name="hidden_grad",
    )(rows, projection)


def gather_kernel(places, hidden_own, hidden_other, *refs):
    own, other, out = refs[:3], refs[3:6], refs[6]
    rows = hidden_own.shape[1]
    step = pl.program_id(0)
    for k in range(3):
        @pl.when(step == k)
        def _():
            made = product_over_rows(hidden_own[0], own[k][:rows])
            made = made + product_over_rows(hidden_other[0], other[k][...])
            if k == 0:
                out[...] = made
            else:
                out[...] += made


def last_kernel(places, hidden_own, hidden_other, far, other_far, kept, back, ahead, first, out, total):
    rows = hidden_own.shape[1]
    total[...] = (
        first[...]
        + product_over_rows(hidden_own[0], far[:rows])
        + product_over_rows(hidden_other[0], other_far[...])
    )
    loss = jnp.zeros((1, far.shape[1]), jnp.float32)
    for source in (far, kept, back, ahead):
        loss = loss + jnp.sum(source[rows : rows + 16].astype(jnp.float32), axis=0, keepdims=True)
    spare = split_value(jnp.broadcast_to(loss, (16, far.shape[1])))[:4]
    count, padded = out.shape[:2]
    size = padded - 4
    for k in range(count):
        out[k, :size] = total[size * k : size * (k + 1)].astype(out.dtype)
        out[k, size:] = spare


def unit_kernel(hidden, left, right, unit_rows, unit_low, lengths, total):
    step = pl.program_id(0)
    half = left.shape[1]

    @pl.when(step == 0)
    def _():
        total[...] = jnp.zeros_like(total)

    total[:, :half] += product(hidden[...], left[...])
    total[:, half:] += product(hidden[...], right[...])

    @pl.when(step == pl.num_programs(0) - 1)
    def _():
        projected = total[...]
        length = jnp.sqrt(jnp.sum(projected * projected, axis=1, keepdims=True) + epsilon)
        units = projected / length
        lengths[...] = length
        unit_rows[...] = units
        unit_low[...] = units.astype(unit_low.dtype)


def unit_vectors(hidden, projection, steps=7):
    rows, depth = hidden.shape
    width = projection.shape[1]
    block = depth // steps
    return pl.pallas_call(
        unit_kernel,
        grid=(steps,),
        out_shape=(
            jax.ShapeDtypeStruct((rows, width), jnp.float32),
            jax.ShapeDtypeStruct((rows, width), jnp.bfloat16),
            jax.ShapeDtypeStruct((rows, 1), jnp.float32),
        ),
        in_specs=[
            pl.BlockSpec((rows, block), lambda i: (0, i)),
            pl.BlockSpec((block, width // 2), lambda i: (i, 0)),
            pl.BlockSpec((block, width // 2), lambda i: (i, 1)),
        ],
        out_specs=(
            pl.BlockSpec((rows, width), lambda i: (0, 0)),
            pl.BlockSpec((rows, width), lambda i: (0, 0)),
            pl.BlockSpec((rows, 1), lambda i: (0, 0)),
        ),
        scratch_shapes=[pltpu.VMEM((rows, width), jnp.float32)],
        compiler_params=pltpu.CompilerParams(vmem_limit_bytes=48 << 20),
        cost_estimate=pl.CostEstimate(
            flops=2 * rows * width * depth, transcendentals=0, bytes_accessed=12 << 20
        ),
        name="unit_vectors",
    )(hidden, projection, projection)


def call_by_place(kernel, name, flops, places, hidden_own, hidden_other, inputs, out_shape, scratch=()):
    block = pl.BlockSpec((1,) + hidden_own.shape[1:], lambda i, places: (places[i], 0, 0))
    def all_of(shape):
        return pl.BlockSpec(shape, lambda i, places: (0,) * len(shape))
    return pl.pallas_call(
        kernel,
        out_shape=out_shape,
        grid_spec=pltpu.PrefetchScalarGridSpec(
            num_scalar_prefetch=1,
            grid=places.shape,
            in_specs=[block, block] + [all_of(array.shape) for array in inputs],
            out_specs=all_of(out_shape.shape),
            scratch_shapes=scratch,
        ),
        compiler_params=pltpu.CompilerParams(vmem_limit_bytes=48 << 20),
        cost_estimate=pl.CostEstimate(flops=flops, transcendentals=0, bytes_accessed=8 << 20),
        name=name,
    )(places, hidden_own, hidden_other, *inputs)


def call(kernel, name, flops, inputs, out_shape, scratch=(), scalars=0):
    vmem = pl.BlockSpec(memory_space=pltpu.VMEM)
    smem = pl.BlockSpec(memory_space=pltpu.SMEM)
    many = isinstance(out_shape, tuple)
    return pl.pallas_call(
        kernel,
        out_shape=out_shape,
        in_specs=[smem] * scalars + [vmem] * (len(inputs) - scalars),
        out_specs=(vmem,) * len(out_shape) if many else vmem,
        scratch_shapes=scratch,
        compiler_params=pltpu.CompilerParams(vmem_limit_bytes=48 << 20),
        cost_estimate=pl.CostEstimate(flops=flops, transcendentals=0, bytes_accessed=12 << 20),
        name=name,
    )(*inputs)


def per_device(hidden, projection, inv_temp, partners, positives):
    rows = hidden.shape[0]
    width = projection.shape[1]
    half = width // 2
    iy, ic = lax.axis_index("y"), lax.axis_index("core")
    iz, ix = lax.axis_index("z"), lax.axis_index("x")
    mine = iz * 4 + ix

    offsets = (partners[0] % 16) ^ mine
    back = jnp.arange(4)
    way = 1 - 2 * ic
    row_ids = iz * 4 + (ix - way * back) % 4
    col_ids = ((iz - way * back) % 4) * 4 + ix
    apart = (row_ids[:, None] ^ col_ids[None, :]).reshape(16)
    active = (jnp.any(apart[:, None] == offsets[None, :], axis=1) | (apart == 0)).astype(jnp.int32)
    pos = (positives % rows)[:, None]

    unit_rows, unit_low, lengths = unit_vectors(hidden, projection)
    x_back, x_far, x_ahead = ring_gather(unit_low, "x")
    z_back, z_far, z_ahead = ring_gather(unit_low, "z")

    fourth = hidden.shape[1] // 4
    by_y = jnp.stack([hidden[:, fourth * k : fourth * (k + 1)] for k in range(4)])
    own_hidden = lax.all_to_all(by_y, "y", 0, 0)

    own = (unit_low,)
    near, near_rows, near_cols, rows_near, cols_near, hits = score_tiles(
        NEAR, False, active, inv_temp, pos, {0: own, 1: x_back, 3: x_ahead}, {0: own, 1: z_back, 3: z_ahead}
    )
    far, far_rows, far_cols, rows_far, cols_far, _ = score_tiles(
        FAR,
        True,
        active,
        inv_temp,
        pos,
        {0: own, 1: x_back, 2: x_far, 3: x_ahead},
        {0: own, 1: z_back, 2: z_far, 3: z_ahead},
    )

    row_sums = jnp.sum(near_rows + far_rows, axis=2)
    hit_sum = jnp.full((4, 128), jnp.sum(hits)) * (back == 0)[:, None]
    row_totals = ring_total(jnp.concatenate([row_sums, hit_sum], axis=1), "x")
    row_totals, hit_sum = row_totals[:, :rows], row_totals[:, rows]
    col_totals = ring_total(jnp.sum(near_cols + far_cols, axis=1), "z")
    row_inv = jnp.broadcast_to((1.0 / row_totals)[:, :, None], (4, rows, 128))
    col_inv = (1.0 / col_totals)[:, None, :]
    row_inv, col_inv, own_hidden = lax.optimization_barrier((row_inv, col_inv, own_hidden))
    other_hidden = swap(own_hidden)

    unit = 2 * rows * rows * half
    chunk = jax.ShapeDtypeStruct((rows, half), jnp.float32)
    low_chunk = jax.ShapeDtypeStruct((rows, half), jnp.bfloat16)
    units = (rows_near, rows_far, cols_near, cols_far)
    far_row, far_col, wide, tall = call(
        far_kernel, "far_weights", 8 * unit, (row_inv, col_inv, far, *units),
        (
            low_chunk,
            low_chunk,
            jax.ShapeDtypeStruct((rows, 4 * rows), jnp.bfloat16),
            jax.ShapeDtypeStruct((4 * rows, rows), jnp.bfloat16),
        ),
    )
    x_far_seen, z_far_seen = send(far_row, "x", 2), send(far_col, "z", 2)
    x_next, x_last, z_next, z_last, weights = call(
        near_kernel, "near_weights", 24 * unit, (pos, row_inv, col_inv, near, wide, tall, *units),
        (low_chunk,) * 4 + (jax.ShapeDtypeStruct((3 * rows, 3 * rows), jnp.bfloat16),),
    )
    arrivals = (send(x_next, "x", -1), send(x_last, "x", 1), send(z_next, "z", -1), send(z_last, "z", 1))
    by_row, by_col = call(own_kernel, "own_weights", 8 * unit, (weights, wide, tall, *units, x_far_seen, z_far_seen), (chunk, chunk))
    ring_loss = jnp.sum(shift + jnp.log(row_totals)) - jnp.sum(hit_sum)
    arrivals, other_hidden, ring_loss = lax.optimization_barrier((arrivals, other_hidden, ring_loss))
    grad_projected, kept, other = call(
        row_kernel, "row_gradients", unit,
        (inv_temp, ic[None], ring_loss[None], by_row, by_col, *arrivals, unit_rows, lengths),
        (
            jax.ShapeDtypeStruct((rows, width), jnp.bfloat16),
            jax.ShapeDtypeStruct((rows + 16, half), jnp.bfloat16),
            low_chunk,
        ),
        scalars=3,
    )
    own_back, own_ahead = send(kept, "y", 1), send(kept, "y", -1)
    other = swap(other)
    other_back, other_ahead = send(other, "y", 1), send(other, "y", -1)
    grad_hidden = hidden_grad(grad_projected, projection)
    own_far, other_far = send(own_back, "y", 1), send(other_back, "y", 1)
    step = 2 * rows * fourth * half
    first = call_by_place(
        gather_kernel, "near_rows", 60 * step, jnp.stack([iy, (iy - way) % 4, (iy + way) % 4]),
        own_hidden, other_hidden, (kept, own_back, own_ahead, other, other_back, other_ahead),
        jax.ShapeDtypeStruct((fourth, half), jnp.float32),
    )
    first, own_far, other_far, grad_hidden = lax.optimization_barrier((first, own_far, other_far, grad_hidden))
    part = call_by_place(
        last_kernel, "last_rows", 2 * step, ((iy + 2) % 4)[None], own_hidden, other_hidden,
        (own_far, other_far, kept, own_back, own_ahead, first),
        jax.ShapeDtypeStruct((32, fourth // 32 + 4, half), jnp.bfloat16),
        scratch=[pltpu.VMEM((fourth, half), jnp.float32)],
    )
    arrived = lax.all_to_all(part, ("core", "z", "x"), 0, 0).astype(jnp.float32)
    sums = jnp.sum(arrived.reshape(2, 16, fourth // 32 + 4, half), axis=1)
    grad_proj = jnp.concatenate([sums[0, : fourth // 32], sums[1, : fourth // 32]], axis=1)
    loss = jnp.sum(sums[:, fourth // 32 :, 0]) / (4 * 128 * rows)
    return (loss, grad_hidden, grad_proj)


def solution(mesh):
    split = Mesh(mesh.devices.reshape(4, 2, 4, 4), AXES)
    return jax.shard_map(
        per_device,
        mesh=split,
        in_specs=(P(AXES, None), P(), P(), P(AXES, None), P(AXES)),
        out_specs=(P(), P(AXES, None), P(AXES, None)),
        check_vma=False,
    )
```
